512 devices in a mesh: section: 8 (over x, y_hi), dp: 64 (over y_lo, z, core).
Axes of the slice: x: 4, y: 4 (y_hi: 2, y_lo: 2; y = y_hi * 2 + y_lo), z: 16, core: 2. Of those that a mesh axis runs over, the one named last changes fastest.
Arguments:
- section_in: bfloat16 [8, 4, 64, 128, 1536], P('section', None, 'dp'), may hold values from -6 to 6
- top_grad: bfloat16 [4, 64, 128, 1536], P(None, 'dp'), may hold values from -0.078125 to 0.078125
- seq_lengths: int32 [4, 64], P(None, 'dp'), may hold values from 32 to 128, as said below
- lang_labels: int32 [4, 64], P(None, 'dp'), may hold values from 0 to 28
- norm_gain: float32 [8, 1536], P('section'), may hold values from 0.5 to 1.5
- w_down: bfloat16 [8, 1536, 256], P('section'), may hold values from -0.15625 to 0.15625
- w_up: bfloat16 [8, 256, 1536], P('section'), may hold values from -0.375 to 0.375
- critic_first: bfloat16 [1536, 768], P('section'), may hold values from -0.15625 to 0.15625
- critic_second: bfloat16 [768, 29], replicated, may hold values from -0.21875 to 0.21875
Outputs:
- grad_w_down: float32 [8, 1536, 256], P('section', 'dp')
- grad_w_up: float32 [8, 256, 1536], P('section', None, 'dp')
- grad_norm_gain: float32 [8, 1536], P('section', 'dp')
- grad_critic_first: float32 [1536, 768], P('section', 'dp')
- grad_critic_second: float32 [768, 29], P('dp')
The draws below stay inside these ranges and needn't reach their ends.
Inputs may be any that keep to these rules, and one draw needn't show every extreme that they name: `seq_lengths`: in every draw some sequence has all 128 tokens valid.
All inputs are finite; a program needn't handle non-finite values.
Results may differ from the reference program's by a relative error of at most 0.023.
Values may be sent and summed in bfloat16 or wider, within the bound.
No kernel may reach another device: no remote copies, remote signals or barrier semaphores. Data moves between devices by JAX's collectives and lax.ppermute only.
A program may use at most 64 MiB of HBM per device.

```python
import jax
import jax.numpy as jnp
from jax import lax

D = 1536
R = 256
CH = 768
NLANG = 29
MICRO = 4
LEN = 128
NSEQ = 64
N_SECTION = 8


def draw_seq_lengths(key, part):
    first_key, second_key = jax.random.split(jax.random.fold_in(key, 11))
    drawn = jax.random.randint(first_key, (MICRO * NSEQ,), LEN // 4, LEN + 1)
    chosen = jax.random.randint(second_key, (), 0, MICRO * NSEQ)
    filled = jnp.where(jnp.arange(MICRO * NSEQ) == chosen, LEN, drawn)
    return filled.reshape(MICRO, NSEQ).astype(jnp.int32)


def set_ends(values, rng, smallest, largest):
    extent = values.shape
    index_at = [jax.random.randint(jax.random.fold_in(rng, axis), (), 0, extent[axis]) for axis in range(len(extent))]
    values = values.at[tuple(index_at)].set(smallest)
    longest = extent.index(max(extent))
    index_at[longest] = (index_at[longest] + 1) % extent[longest]
    return values.at[tuple(index_at)].set(largest)


def strengthened(values, rng, source, target, shards_of, factor):
    owner, partner = [(jnp.arange(values.shape[dim]) // (values.shape[dim] // shards_of)).reshape([-1 if axis == dim else 1 for axis in range(values.ndim)]) for dim in (source, target)]
    chosen = jax.random.permutation(rng, shards_of)[partner]
    strong = (owner == chosen) | (owner == (partner + shards_of // 2) % shards_of)
    return jnp.where(strong, factor * values, values)


def shard_levels(stream_key, dims, shards, least, top_value):
    def one(dim, blocks):
        draws = jax.random.uniform(jax.random.fold_in(jax.random.fold_in(stream_key, 6), dim), (blocks,), jnp.float32, least / len(shards), top_value / len(shards))
        return jnp.repeat(jnp.exp(draws), dims[dim] // blocks).reshape((-1,) + (1,) * (len(dims) - dim - 1))

    loudness = one(*shards[0])
    for cut in shards[1:]:
        loudness = loudness * one(*cut)
    return loudness


def noise(own_key, dims, scale, most, cuts=(), held_as=jnp.bfloat16):
    level = shard_levels(own_key, dims, cuts, -0.22, 0.18) if cuts else 1.0
    values = jax.random.normal(own_key, dims, jnp.float32) * scale * level
    return jnp.minimum(jnp.maximum(values, -most), most).astype(held_as)


def gaussian_with(own_key, extent, deviation, limit, pieces, heavy, dtype=jnp.bfloat16):
    result = deviation * jax.random.normal(own_key, extent, jnp.float32)
    if pieces:
        result = result * shard_levels(own_key, extent, pieces, -0.22, 0.18)
    return jnp.clip(strengthened(result, jax.random.fold_in(own_key, 3), *heavy), -limit, limit).astype(dtype)


def setup_inputs(seed: int = 0) -> dict:
    arg_keys = jax.random.split(jax.random.key(seed), 10)
    return {
        "section_in": noise(arg_keys[0], (N_SECTION, MICRO, NSEQ, LEN, D), 1.0, 6.0, ((0, 8), (2, 64))),
        "top_grad": gaussian_with(arg_keys[1], (MICRO, NSEQ, LEN, D), 0.005, 0.078125, ((1, 64),), (1, 3, 64, 4.0)),
        "seq_lengths": draw_seq_lengths(jax.random.fold_in(arg_keys[9], 71), 0),
        "lang_labels": set_ends(jax.random.randint(arg_keys[3], (MICRO, NSEQ), 0, NLANG), jax.random.fold_in(arg_keys[3], 1), 0, NLANG - 1).astype(jnp.int32),
        "norm_gain": jnp.clip(1.0 + 0.1 * jax.random.normal(arg_keys[4], (N_SECTION, D), jnp.float32), 0.5, 1.5),
        "w_down": noise(arg_keys[5], (N_SECTION, D, R), D ** -0.5, 0.15625, ((0, 8),)),
        "w_up": noise(arg_keys[6], (N_SECTION, R, D), R ** -0.5, 0.375, ((0, 8),)),
        "critic_first": noise(arg_keys[7], (D, CH), D ** -0.5, 0.15625, ((0, 8),)),
        "critic_second": noise(arg_keys[8], (CH, NLANG), CH ** -0.5, 0.21875),
    }


EPSILON = 1e-06
REVERSAL = 0.5

def silu_slope(pre_act):
    sigma = jax.nn.sigmoid(pre_act)
    return sigma * (1.0 + pre_act * (1.0 - sigma))

def inner_rows(left, right):
    return lax.dot_general(left, right, (((0,), (0,)), ((), ())), preferred_element_type=jnp.float32)

def adapter_backward(local_rows, upstream, gain_row, down_proj, up_proj):
    values = local_rows.astype(jnp.float32)
    inv_rms = lax.rsqrt(lax.optimization_barrier(jnp.mean(values * values, axis=-1, keepdims=True)) + EPSILON)
    unit_rows = values * inv_rms
    normed = (unit_rows * gain_row[None, :]).astype(jnp.bfloat16)
    pre_act = jnp.dot(normed, down_proj, preferred_element_type=jnp.float32)
    hidden = jax.nn.silu(pre_act).astype(jnp.bfloat16)
    grad_up = inner_rows(hidden, upstream)
    grad_hidden = jnp.dot(upstream, up_proj.T, preferred_element_type=jnp.float32)
    grad_pre = (grad_hidden * silu_slope(pre_act)).astype(jnp.bfloat16)
    grad_down = inner_rows(normed, grad_pre)
    grad_normed = jnp.dot(grad_pre, down_proj.T, preferred_element_type=jnp.float32)
    grad_gain = lax.optimization_barrier(jnp.sum(grad_normed * unit_rows, axis=0))
    scaled = grad_normed * gain_row[None, :]
    grad_input = upstream.astype(jnp.float32) + inv_rms * (scaled - unit_rows * lax.optimization_barrier(jnp.mean(scaled * unit_rows, axis=-1, keepdims=True)))
    return (grad_input, grad_down, grad_up, grad_gain)

def reference(section_in, top_grad, seq_lengths, lang_labels, norm_gain, w_down, w_up, critic_first, critic_second):
    target = N_SECTION // 2
    positions = jnp.arange(LEN)
    valid_mask = (positions[None, None, :] < seq_lengths[:, :, None]).astype(jnp.float32)
    lengths = seq_lengths.astype(jnp.float32)
    totals = jnp.einsum('mnt,mntd->mnd', valid_mask, section_in[target].astype(jnp.float32))
    pooled = (totals / lengths[:, :, None]).astype(jnp.bfloat16)
    batch_rows = MICRO * NSEQ
    values = pooled.reshape(batch_rows, D).astype(jnp.float32)
    inv_rms = lax.rsqrt(lax.optimization_barrier(jnp.mean(values * values, axis=-1, keepdims=True)) + EPSILON)
    unit_rows = values * inv_rms
    normed = unit_rows.astype(jnp.bfloat16)
    pre_act = jnp.dot(normed, critic_first, preferred_element_type=jnp.float32)
    hidden = jax.nn.silu(pre_act).astype(jnp.bfloat16)
    logits = jnp.dot(hidden, critic_second, preferred_element_type=jnp.float32)
    exponent = jnp.exp(logits)
    probabilities = exponent / lax.optimization_barrier(jnp.sum(exponent, axis=-1, keepdims=True))
    onehot = (lang_labels.reshape(batch_rows)[:, None] == jnp.arange(NLANG)[None, :]).astype(jnp.float32)
    grad_logits = (probabilities - onehot).astype(jnp.bfloat16)
    grad_second = inner_rows(hidden, grad_logits)
    grad_hidden = jnp.dot(grad_logits, critic_second.T, preferred_element_type=jnp.float32)
    grad_pre = (grad_hidden * silu_slope(pre_act)).astype(jnp.bfloat16)
    grad_first = inner_rows(normed, grad_pre)
    grad_normed = jnp.dot(grad_pre, critic_first.T, preferred_element_type=jnp.float32)
    grad_pooled = inv_rms * (grad_normed - unit_rows * lax.optimization_barrier(jnp.mean(grad_normed * unit_rows, axis=-1, keepdims=True)))
    reversal = (-REVERSAL * grad_pooled / lengths.reshape(batch_rows)[:, None]).reshape(MICRO, NSEQ, D)
    down_sums = [jnp.zeros((D, R), jnp.float32) for level in range(N_SECTION)]
    up_sums = [jnp.zeros((R, D), jnp.float32) for level in range(N_SECTION)]
    gain_sums = [jnp.zeros((D,), jnp.float32) for level in range(N_SECTION)]
    for micro_index in range(MICRO):
        upstream = top_grad[micro_index].reshape(NSEQ * LEN, D)
        for level in reversed(range(N_SECTION)):
            local_rows = section_in[level, micro_index].reshape(NSEQ * LEN, D)
            grad_input, grad_down, grad_up, grad_gain = adapter_backward(local_rows, upstream, norm_gain[level], w_down[level], w_up[level])
            down_sums[level] = down_sums[level] + grad_down
            up_sums[level] = up_sums[level] + grad_up
            gain_sums[level] = gain_sums[level] + grad_gain
            if level == target:
                extra = reversal[micro_index][:, None, :] * valid_mask[micro_index][:, :, None]
                grad_input = grad_input + extra.reshape(NSEQ * LEN, D)
            upstream = grad_input.astype(jnp.bfloat16)
    return (jnp.stack(down_sums), jnp.stack(up_sums), jnp.stack(gain_sums), grad_first, grad_second)
```

```python
import functools

import jax
import jax.numpy as jnp
from jax import lax
from jax.experimental import pallas as pl
from jax.experimental.pallas import tpu as pltpu
from jax.sharding import Mesh, PartitionSpec as P


EPSILON = 1e-06
REVERSAL = 0.5
SECTIONS = 8
CHUNK = 64
DELAY = 2
SEC = ("x", "yh")
F32 = jnp.float32
BF16 = jnp.bfloat16
VM = pl.BlockSpec(memory_space=pltpu.VMEM)
SM = pl.BlockSpec(memory_space=pltpu.SMEM)


def silu_slope(pre_act):
    sigma = jax.nn.sigmoid(pre_act)
    return sigma * (1.0 + pre_act * (1.0 - sigma))


def call(kernel, out_shape, in_specs, args, flops, moved, aliases=None, scratch=(), limit=24):
    return pl.pallas_call(
        kernel,
        out_shape=out_shape,
        in_specs=in_specs,
        out_specs=jax.tree.map(lambda _: VM, out_shape),
        input_output_aliases=aliases or {},
        scratch_shapes=scratch,
        compiler_params=pltpu.CompilerParams(vmem_limit_bytes=limit << 20),
        cost_estimate=pl.CostEstimate(flops=flops, bytes_accessed=moved, transcendentals=0),
    )(*args)


def prepare_kernel(
    lens_ref, core_ref, _labels, x_ref, gain_ref, wd_ref, wu_ref, first_ref, low_ref, xn_ref, h_ref, a_ref, q_ref, pooled_ref, wut_ref, wdt_ref, mine_ref, second_ref, _g, _da
):
    micros, seq_len = 4, 128
    gain = gain_ref[0:1, :]
    half = first_ref.shape[1] // 2
    for c in range(2):

        @pl.when(core_ref[0] == c)
        def _():
            mine_ref[...] = first_ref[:, c * half : (c + 1) * half]

    second_ref[...] = low_ref[...]
    wut_ref[...] = wu_ref[...].T
    wdt_ref[...] = wd_ref[...].T
    pooled_ref[...] = jnp.zeros_like(pooled_ref)
    positions = lax.broadcasted_iota(jnp.int32, (seq_len, 1), 0)
    for m in range(micros):
        rows = pl.ds(m * seq_len, seq_len)
        values = x_ref[rows, :].astype(F32)
        count = lens_ref[m, 0]
        total = jnp.sum(jnp.where(positions < count, values, 0.0), axis=0, keepdims=True)
        pooled_ref[m : m + 1, :] = total / count.astype(F32)
        q = lax.rsqrt(jnp.mean(values * values, axis=-1, keepdims=True) + EPSILON)
        normed = (values * q * gain).astype(BF16)
        xn_ref[rows, :] = normed
        a = jnp.dot(normed, wd_ref[...], preferred_element_type=F32)
        a_ref[rows, :] = a
        h_ref[rows, :] = (a * jax.nn.sigmoid(a)).astype(BF16)
        q_ref[rows, :] = jnp.broadcast_to(q, (seq_len, 128))


def step_kernel(step, chunks, has_top, has_in, has_rev, *refs):
    refs = list(refs)
    sec_ref, lens_ref, x_ref, a_ref, q_ref, gain_ref, wut_ref, wdt_ref = refs[:8]
    refs = refs[8:]
    top_ref = refs.pop(0) if has_top else None
    in_ref = refs.pop(0) if has_in else None
    rev_ref = refs.pop(0) if has_rev else None
    _, _, out_ref, g_ref, da_ref = refs
    features = x_ref.shape[1]
    sec = sec_ref[0]
    place = step - DELAY * (SECTIONS - 1 - sec)
    live = (place >= 0) & (place < chunks)
    place = jnp.clip(place, 0, chunks - 1)
    rows = pl.ds(pl.multiple_of(place * CHUNK, CHUNK), CHUNK)

    if has_top:

        @pl.when(live & (sec == SECTIONS - 1))
        def _():
            g_ref[rows, :] = top_ref[rows, :]

    if has_in:

        @pl.when(live & (sec < SECTIONS - 1))
        def _():
            g_ref[rows, :] = in_ref[...]

    if has_rev:

        @pl.when(live & (sec == SECTIONS // 2 - 1))
        def _():
            per = 128 // CHUNK
            micro = lax.div(place, per)
            first = lax.rem(place, per) * CHUNK
            positions = lax.broadcasted_iota(jnp.int32, (CHUNK, 1), 0) + first
            extra = jnp.where(positions < lens_ref[micro, 0], rev_ref[pl.ds(micro, 1), :], 0.0)
            g_ref[rows, :] = (in_ref[...].astype(F32) + extra).astype(BF16)

    @pl.when(live)
    def _():
        g = g_ref[rows, :]
        a = a_ref[rows, :]
        q = q_ref[rows, 0:1]
        dh = jnp.dot(g, wut_ref[...], preferred_element_type=F32)
        da = (dh * silu_slope(a)).astype(BF16)
        da_ref[rows, :] = da
        mean = jnp.sum(da.astype(F32) * a, axis=-1, keepdims=True) * (1.0 / features)
        dxn = jnp.dot(da, wdt_ref[...], preferred_element_type=F32)
        x = x_ref[rows, :].astype(F32)
        out = g.astype(F32) + q * (dxn * gain_ref[0:1, :]) - x * (q * q * mean)
        out_ref[...] = out.astype(BF16)


def per_row(ref, shape):
    rows = lax.broadcasted_iota(jnp.int32, shape, 0)
    column = jnp.ones(shape, jnp.int32)
    for m in range(4):
        column = jnp.where(rows == m, ref[m, 0], column)
    return column


def critic_kernel(
    sec_ref, core_ref, labels_ref, lens_ref, pooled_ref, own_ref, other_ref, second_ref, lines_ref, rev_ref, hold
):
    half = own_ref.shape[1]
    channels = 2 * half
    languages = second_ref.shape[1]

    @pl.when(sec_ref[0] == SECTIONS // 2 - 1)
    def _():
        pooled = pooled_ref[...].astype(BF16).astype(F32)
        r = lax.rsqrt(jnp.mean(pooled * pooled, axis=-1, keepdims=True) + EPSILON)
        unit = pooled * r
        normed = unit.astype(BF16)
        core = core_ref[0]
        pre_own = jnp.dot(normed, own_ref[...], preferred_element_type=F32)
        pre_other = jnp.dot(normed, other_ref[...], preferred_element_type=F32)
        low = jnp.where(core == 0, pre_own, pre_other)
        high = jnp.where(core == 0, pre_other, pre_own)
        pre = jnp.concatenate([low, high], axis=1)
        hidden = (pre * jax.nn.sigmoid(pre)).astype(BF16)
        second = second_ref[...]
        logits = jnp.dot(hidden, second, preferred_element_type=F32)
        exponent = jnp.exp(logits)
        probs = exponent / jnp.sum(exponent, axis=-1, keepdims=True)
        lanes = lax.broadcasted_iota(jnp.int32, logits.shape, 1)
        onehot = jnp.where(lanes == per_row(labels_ref, logits.shape), 1.0, 0.0)
        valid = lax.broadcasted_iota(jnp.int32, logits.shape, 0) < 4
        grad_logits = jnp.where(valid, probs - onehot, 0.0).astype(BF16)
        dims = (((1,), (1,)), ((), ()))
        grad_hidden = lax.dot_general(grad_logits, second, dims, preferred_element_type=F32)
        grad_pre = (grad_hidden * silu_slope(pre)).astype(BF16)
        hold[...] = jnp.zeros_like(hold)
        hold[0:8, :] = normed.astype(F32)
        hold[8:16, 0:channels] = grad_pre.astype(F32)
        hold[8:16, channels:] = hidden.astype(F32)
        hold[16:24, 0:languages] = grad_logits.astype(F32)
        lines_ref[...] = hold[...].astype(BF16)
        low = grad_pre[:, :half]
        high = grad_pre[:, half:]
        mine = jnp.where(core == 0, low, high)
        theirs = jnp.where(core == 0, high, low)
        grad_normed = lax.dot_general(mine, own_ref[...], dims, preferred_element_type=F32)
        grad_normed += lax.dot_general(theirs, other_ref[...], dims, preferred_element_type=F32)
        mean = jnp.mean(grad_normed * unit, axis=-1, keepdims=True)
        grad_pooled = r * (grad_normed - unit * mean)
        rev_ref[...] = -REVERSAL * grad_pooled / per_row(lens_ref, (8, 1)).astype(F32)


def unpack_kernel(sec_ref, band_rows, n_dp, lines_ref, nb_ref, gp_ref, hid_ref, gl_ref):
    features = lines_ref.shape[1]
    channels = features // 2
    padded = gp_ref.shape[1] // n_dp
    share = channels // n_dp

    def grow(block):
        return jnp.concatenate([block, jnp.zeros_like(block)], axis=0).astype(BF16)

    def pick(shape, test):
        rows = lax.broadcasted_iota(jnp.int32, shape, 0)
        columns = lax.broadcasted_iota(jnp.int32, shape, 1)
        return jnp.where(test(rows, columns), 1.0, 0.0).astype(BF16)

    lines = lines_ref[...].astype(F32)
    base = sec_ref[0] * band_rows
    band = pick((features, 256), lambda i, j: (i == j + base) & (j < band_rows))
    nb_ref[...] = jnp.dot(grow(lines[0:8]), band, preferred_element_type=F32).astype(BF16)
    wide = (channels, n_dp * padded)
    columns = lax.broadcasted_iota(jnp.int32, (1, wide[1]), 1)
    slot = lax.div(columns, padded)
    inside = columns - slot * padded
    source = jnp.where(inside < share, slot * share + inside, -1)
    spread = jnp.where(lax.broadcasted_iota(jnp.int32, wide, 0) == source, 1.0, 0.0).astype(BF16)
    both = grow(lines[8:16])
    gp_ref[...] = jnp.dot(both[:, :channels], spread, preferred_element_type=F32).astype(BF16)
    hid_ref[...] = jnp.dot(both[:, channels:], spread, preferred_element_type=F32).astype(BF16)
    shift = pick((128, 128), lambda i, j: j == i + 64)
    gl_ref[...] = jnp.dot(grow(lines[16:24, :128]), shift, preferred_element_type=F32).astype(BF16)


def finish_kernel(parts, place_ref, xn_ref, g_ref, h_ref, da_ref, nb_ref, gl_ref, gp_ref, hid_ref, *refs):
    outs, (down, up, crit) = refs[:-3], refs[-3:]
    n_yl, n_z, n_c = parts
    features = xn_ref.shape[1]
    dims = (((0,), (0,)), ((), ()))
    width = 256
    for k in range(features // width):
        cols = pl.ds(k * width, width)
        down[cols, :] = lax.dot_general(xn_ref[:, cols], da_ref[...], dims, preferred_element_type=F32)
        up[cols, :] = lax.dot_general(g_ref[:, cols], h_ref[...], dims, preferred_element_type=F32)
    crit[:, :128] = lax.dot_general(gp_ref[...], nb_ref[:, :128], dims, preferred_element_type=F32)
    crit[:, 128:] = lax.dot_general(
        gp_ref[...], nb_ref[:, 128:], dims, preferred_element_type=F32
    ) + lax.dot_general(hid_ref[...], gl_ref[...], dims, preferred_element_type=F32)
    span = features // (n_yl * n_z * n_c)
    cspan = crit.shape[0] // (n_yl * n_z * n_c)
    my_yl, my_c = place_ref[0], place_ref[1]

    def pack(z, _):
        for dy in range(n_yl):
            for dc in range(n_c):
                yl = my_yl if dy == 0 else n_yl - 1 - my_yl
                c = my_c if dc == 0 else n_c - 1 - my_c
                dest = (yl * n_z + z) * n_c + c
                wide = pl.ds(pl.multiple_of(dest * span, 8), span)
                thin = pl.ds(pl.multiple_of(dest * cspan, 8), cspan)
                piece = jnp.concatenate([down[wide, :], up[wide, :], crit[thin, :]], axis=0)
                outs[dc * n_yl + dy][z] = piece.astype(BF16)
        return 0

    lax.fori_loop(0, n_z, pack, 0)


def join_kernel(sec_ref, *refs):
    *parts, out_ref = refs
    rows = parts[0].shape[0]

    @pl.when(sec_ref[0] % 2 == 1)
    def _():
        for i, ref in enumerate(parts):
            out_ref[i * rows : (i + 1) * rows, :] = ref[...]


def after(value, token):
    return lax.optimization_barrier((value, token))[0]


def swap(block, axis, size):
    return lax.ppermute(block, axis, [(i, size - 1 - i) for i in range(size)])


def body(parts, *args):
    return whole(parts, *args)


def whole(parts, section_in, top_grad, seq_lengths, lang_labels, norm_gain, w_down, w_up, critic_first, critic_second):
    n_yl, n_z, n_c = parts
    n_dp = n_yl * n_z * n_c
    sec = lax.axis_index(SEC)
    core = lax.axis_index("c")
    micros, seq_len, features = 4, 128, section_in.shape[-1]
    rank = w_down.shape[-1]
    rows = micros * seq_len
    chunks = rows // CHUNK
    x = section_in.reshape(rows, features)
    top = top_grad.reshape(rows, features)
    gain = norm_gain.reshape(1, features)
    wd = w_down[0]
    sec_s = sec.reshape(1).astype(jnp.int32)
    core_s = core.reshape(1).astype(jnp.int32)
    channels = critic_first.shape[1]
    half = channels // 2
    sds = jax.ShapeDtypeStruct

    xn, h, a, q, pooled, wut, wdt, mine, second, grads, inner = call(
        prepare_kernel,
        (
            sds((rows, features), BF16),
            sds((rows, rank), BF16),
            sds((rows, rank), F32),
            sds((rows, 128), F32),
            sds((8, features), F32),
            sds((features, rank), BF16),
            sds((rank, features), BF16),
            sds((critic_first.shape[0], half), BF16),
            sds(critic_second.shape, BF16),
            sds((rows, features), BF16),
            sds((rows, rank), BF16),
        ),
        [SM] * 3 + [VM] * 6,
        (seq_lengths, core_s, lang_labels, x, gain, wd, w_up[0], critic_first, critic_second),
        2 * rows * features * rank,
        8 << 20,
        limit=10,
    )

    three = SECTIONS // 2 - 1
    held = {}
    band_rows = critic_first.shape[0]
    share = channels // n_dp
    padded = -(-share // 16) * 16

    def join(token, *pieces):
        return call(
            join_kernel,
            sds((len(pieces) * pieces[0].shape[0], half), BF16),
            [SM] + [VM] * len(pieces),
            (after(sec_s, token), *pieces),
            0,
            2 << 20,
            limit=4,
        )

    def side_work(step, token):
        if step == 0:
            held["even"] = lax.ppermute(after(mine, token), SEC, [(i, i + 1) for i in range(0, SECTIONS, 2)])
        elif step == 1:
            held["pooled"] = lax.ppermute(after(pooled, token), SEC, [(4, three)])
        elif step == 2:
            held["pair"] = join(token, held["even"], mine)
            held["far"] = [lax.ppermute(held["pair"], SEC, [(i, three)]) for i in (1, 5, 7)]
        elif step == 5:
            held["own"] = join(token, held["far"][0], held["pair"], *held["far"][1:])
            pairs = [(three * 2, three * 2 + 1), (three * 2 + 1, three * 2)]
            held["other"] = lax.ppermute(held["own"], SEC + ("c",), pairs)
        elif step == 7:
            held["lines"], held["rev"] = call(
                critic_kernel,
                (sds((32, features), BF16), sds((8, features), F32)),
                [SM] * 4 + [VM] * 4,
                (
                    after(sec_s, token),
                    core_s,
                    lang_labels,
                    seq_lengths,
                    held["pooled"],
                    held["own"],
                    held["other"],
                    second,
                ),
                1 << 27,
                4 << 20,
                scratch=[pltpu.VMEM((32, features), F32)],
                limit=8,
            )
        elif step in (9, 12, 15):
            lines = after(held["lines"], token)
            if step == 9:
                moved = lax.ppermute(lines, SEC, [(3, 7)])
                gets = sec == 7
            elif step == 12:
                moved = lax.ppermute(lines, SEC, [(3, 1), (7, 5)])
                gets = (sec == 1) | (sec == 5)
            else:
                moved = lax.ppermute(lines, SEC, [(i + 1, i) for i in range(0, SECTIONS, 2)])
                gets = sec % 2 == 0
            held["lines"] = jnp.where(gets, moved, lines)
        elif step == 18:
            held["critic"] = call(
                lambda sec_ref, *refs: unpack_kernel(sec_ref, band_rows, n_dp, *refs),
                (
                    sds((16, 256), BF16),
                    sds((16, n_dp * padded), BF16),
                    sds((16, n_dp * padded), BF16),
                    sds((16, 128), BF16),
                ),
                [SM, VM],
                (after(sec_s, token), held["lines"]),
                1 << 26,
                1 << 20,
                limit=12,
            )

    steps = DELAY * (SECTIONS - 1) + chunks
    received = {}
    route = [(i, i - 1) for i in range(1, SECTIONS)]
    for step in range(steps):
        has_top = step < chunks
        has_in = step >= DELAY
        first_rev = DELAY * (SECTIONS - 1 - three)
        has_rev = first_rev <= step < first_rev + chunks
        args = [sec_s, seq_lengths, x, a, q, gain, wut, wdt]
        specs = [SM, SM] + [VM] * 6
        if has_top:
            args.append(top)
        if has_in:
            args.append(received.pop(step - DELAY))
        if has_rev:
            args.append(held["rev"])
        args += [grads, inner]
        specs += [VM] * (len(args) - len(specs))
        outgoing, grads, inner = call(
            functools.partial(step_kernel, step, chunks, has_top, has_in, has_rev),
            (sds((CHUNK, features), BF16), sds((rows, features), BF16), sds((rows, rank), BF16)),
            specs,
            tuple(args),
            4 * CHUNK * features * rank,
            3 << 20,
            aliases={len(args) - 2: 1, len(args) - 1: 2},
            limit=6,
        )
        if step < steps - DELAY:
            received[step] = lax.ppermute(outgoing, SEC, route)
        side_work(step, outgoing)

    band, gp, hid, gl = held["critic"]
    span = features // n_dp
    piece = sds((n_z, 2 * span + padded, rank), BF16)
    place = jnp.stack([lax.axis_index("yl"), core]).astype(jnp.int32)
    packed = call(
        functools.partial(finish_kernel, parts),
        (piece,) * (n_yl * n_c),
        [SM] + [VM] * 8,
        (place, xn, grads, h, inner, band, gl, gp, hid),
        4 * rows * features * rank,
        8 << 20,
        scratch=[pltpu.VMEM((features, rank), F32)] * 2 + [pltpu.VMEM((n_dp * padded, rank), F32)],
        limit=16,
    )

    def add(left, right):
        return (left.astype(F32) + right.astype(F32)).astype(BF16)

    kept, sent = packed[:n_yl], packed[n_yl:]
    halves = [None] * n_yl
    for i in reversed(range(n_yl)):
        halves[i] = add(kept[i], swap(sent[i], "c", n_c))
    summed = halves[0]
    if n_yl == 2:
        summed = add(summed, swap(halves[1], "yl", n_yl))
    if n_z > 1:
        summed = lax.all_to_all(summed, "z", 0, 0, tiled=True)
    total = jnp.sum(summed.astype(F32), axis=0)
    down = total[:span]
    up = total[span : 2 * span].T
    crit = total[2 * span : 2 * span + share]
    dp_place = lax.axis_index(("yl", "z", "c"))
    wd_own = lax.dynamic_slice_in_dim(wd, dp_place * span, span, 0).astype(F32)
    gain_own = lax.dynamic_slice_in_dim(gain[0], dp_place * span, span, 0)
    grad_gain = jnp.sum(down * wd_own, axis=1) / gain_own
    first = crit[:, :band_rows].T
    second_grad = crit[:, 192 : 192 + critic_second.shape[1]]
    return (down[None], up[None], grad_gain[None], first, second_grad)


def solution(mesh):
    n_dp = mesh.shape["dp"]
    parts = (2, n_dp // 4, 2) if n_dp >= 8 else (1, n_dp // 2, 2)
    fine = Mesh(mesh.devices.reshape((SECTIONS // 2, 2) + parts), SEC + ("yl", "z", "c"))
    dp = ("yl", "z", "c")
    return jax.shard_map(
        functools.partial(body, parts),
        mesh=fine,
        in_specs=(
            P(SEC, None, dp, None, None),
            P(None, dp, None, None),
            P(None, dp),
            P(None, dp),
            P(SEC, None),
            P(SEC, None, None),
            P(SEC, None, None),
            P(SEC, None),
            P(),
        ),
        out_specs=(P(SEC, dp, None), P(SEC, None, dp), P(SEC, dp), P(SEC, dp), P(dp, None)),
        check_vma=False,
    )
```

```python
import functools

import jax
import jax.numpy as jnp
from jax import lax
from jax.experimental import pallas as pl
from jax.experimental.pallas import tpu as pltpu
from jax.sharding import Mesh, PartitionSpec as P


EPSILON = 1e-06
REVERSAL = 0.5
SECTIONS = 8
CHUNK = 64
DELAY = 2
SEC = ("x", "yh")
F32 = jnp.float32
BF16 = jnp.bfloat16
VM = pl.BlockSpec(memory_space=pltpu.VMEM)
SM = pl.BlockSpec(memory_space=pltpu.SMEM)
HB = pl.BlockSpec(memory_space=pltpu.MemorySpace.HBM)


def silu_slope(pre_act):
    sigma = jax.nn.sigmoid(pre_act)
    return sigma * (1.0 + pre_act * (1.0 - sigma))


def call(kernel, out_shape, in_specs, args, flops, moved, aliases=None, scratch=(), limit=16):
    return pl.pallas_call(
        kernel,
        out_shape=out_shape,
        in_specs=in_specs,
        out_specs=jax.tree.map(lambda _: VM, out_shape),
        input_output_aliases=aliases or {},
        scratch_shapes=scratch,
        compiler_params=pltpu.CompilerParams(vmem_limit_bytes=limit << 20),
        cost_estimate=pl.CostEstimate(flops=flops, bytes_accessed=moved, transcendentals=0),
    )(*args)


def half_kernel(core_ref, first_ref, mine_ref, sem):
    half = mine_ref.shape[1]
    columns = pl.ds(pl.multiple_of(core_ref[0] * half, 128), half)
    copy = pltpu.make_async_copy(first_ref.at[:, columns], mine_ref, sem)
    copy.start()
    copy.wait()


def prepare_kernel(lens_ref, *refs):
    sources, refs = refs[:6], refs[6:]
    x_ref, top_ref, gain_ref, second_ref, xn_ref, h_ref, a_ref, q_ref, pooled_ref, wut_ref, wdt_ref, _, _ = refs[:13]
    wd_ref, wu_ref, sems = refs[13:]
    x_hbm, top_hbm, gain_hbm, second_hbm, wd_hbm, wu_hbm = sources
    micros, seq_len = 4, 128
    pairs = [(wd_hbm, wd_ref), (gain_hbm, gain_ref), (wu_hbm, wu_ref), (second_hbm, second_ref), (top_hbm, top_ref)]
    for m in range(micros):
        rows = slice(m * seq_len, (m + 1) * seq_len)
        pairs.append((x_hbm.at[rows], x_ref.at[rows]))
    copies = [pltpu.make_async_copy(source, target, sems.at[i]) for i, (source, target) in enumerate(pairs)]
    for i in (0, 1, 5, 6, 7, 8, 2, 3, 4):
        copies[i].start()
    copies[0].wait()
    copies[1].wait()
    gain = gain_ref[0:1, :]
    wdt_ref[...] = wd_ref[...].T
    pooled_ref[...] = jnp.zeros_like(pooled_ref)
    positions = lax.broadcasted_iota(jnp.int32, (seq_len, 1), 0)
    for m in range(micros):
        copies[5 + m].wait()
        rows = pl.ds(m * seq_len, seq_len)
        values = x_ref[rows, :].astype(F32)
        count = lens_ref[m]
        total = jnp.sum(jnp.where(positions < count, values, 0.0), axis=0, keepdims=True)
        pooled_ref[m : m + 1, :] = total / count.astype(F32)
        q = lax.rsqrt(jnp.mean(values * values, axis=-1, keepdims=True) + EPSILON)
        normed = (values * q * gain).astype(BF16)
        xn_ref[rows, :] = normed
        a = jnp.dot(normed, wd_ref[...], preferred_element_type=F32)
        a_ref[rows, :] = a
        h_ref[rows, :] = (a * jax.nn.sigmoid(a)).astype(BF16)
        q_ref[rows, :] = jnp.broadcast_to(q, (seq_len, 128))
    copies[2].wait()
    wut_ref[...] = wu_ref[...].T
    copies[3].wait()
    copies[4].wait()


def step_kernel(step, chunks, has_top, has_in, has_rev, *refs):
    refs = list(refs)
    sec_ref, lens_ref, x_ref, a_ref, q_ref, gain_ref, wut_ref, wdt_ref = refs[:8]
    refs = refs[8:]
    top_ref = refs.pop(0) if has_top else None
    in_ref = refs.pop(0) if has_in else None
    rev_ref = refs.pop(0) if has_rev else None
    _, _, out_ref, g_ref, da_ref = refs
    features = x_ref.shape[1]
    sec = sec_ref[0]
    place = step - DELAY * (SECTIONS - 1 - sec)
    live = (place >= 0) & (place < chunks)
    place = jnp.clip(place, 0, chunks - 1)
    rows = pl.ds(pl.multiple_of(place * CHUNK, CHUNK), CHUNK)

    if has_top:

        @pl.when(live & (sec == SECTIONS - 1))
        def _():
            g_ref[rows, :] = top_ref[rows, :]

    if has_in:

        @pl.when(live & (sec < SECTIONS - 1))
        def _():
            g_ref[rows, :] = in_ref[...]

    if has_rev:

        @pl.when(live & (sec == SECTIONS // 2 - 1))
        def _():
            per = 128 // CHUNK
            micro = lax.div(place, per)
            first = lax.rem(place, per) * CHUNK
            positions = lax.broadcasted_iota(jnp.int32, (CHUNK, 1), 0) + first
            extra = jnp.where(positions < lens_ref[micro], rev_ref[pl.ds(micro, 1), :], 0.0)
            g_ref[rows, :] = (in_ref[...].astype(F32) + extra).astype(BF16)

    @pl.when(live)
    def _():
        g = g_ref[rows, :]
        a = a_ref[rows, :]
        q = q_ref[rows, 0:1]
        dh = jnp.dot(g, wut_ref[...], preferred_element_type=F32)
        da = (dh * silu_slope(a)).astype(BF16)
        da_ref[rows, :] = da
        mean = jnp.sum(da.astype(F32) * a, axis=-1, keepdims=True) * (1.0 / features)
        dxn = jnp.dot(da, wdt_ref[...], preferred_element_type=F32)
        x = x_ref[rows, :].astype(F32)
        out = g.astype(F32) + q * (dxn * gain_ref[0:1, :]) - x * (q * q * mean)
        out_ref[...] = out.astype(BF16)


def per_row(ref, shape):
    rows = lax.broadcasted_iota(jnp.int32, shape, 0)
    column = jnp.ones(shape, jnp.int32)
    for m in range(4):
        column = jnp.where(rows == m, ref[m], column)
    return column


def critic_kernel(
    sec_ref, core_ref, labels_ref, lens_ref, pooled_ref, own_ref, other_ref, second_ref, lines_ref, rev_ref, hold
):
    half = own_ref.shape[1]
    channels = 2 * half
    languages = second_ref.shape[0]

    @pl.when(sec_ref[0] == SECTIONS // 2 - 1)
    def _():
        pooled = pooled_ref[...].astype(BF16).astype(F32)
        r = lax.rsqrt(jnp.mean(pooled * pooled, axis=-1, keepdims=True) + EPSILON)
        unit = pooled * r
        normed = unit.astype(BF16)
        core = core_ref[0]
        pre_own = jnp.dot(normed, own_ref[...], preferred_element_type=F32)
        pre_other = jnp.dot(normed, other_ref[...], preferred_element_type=F32)
        low = jnp.where(core == 0, pre_own, pre_other)
        high = jnp.where(core == 0, pre_other, pre_own)
        pre = jnp.concatenate([low, high], axis=1)
        hidden = (pre * jax.nn.sigmoid(pre)).astype(BF16)
        second = second_ref[...]
        dims = (((1,), (1,)), ((), ()))
        logits = lax.dot_general(hidden, second, dims, preferred_element_type=F32)
        exponent = jnp.exp(logits)
        probs = exponent / jnp.sum(exponent, axis=-1, keepdims=True)
        lanes = lax.broadcasted_iota(jnp.int32, logits.shape, 1)
        onehot = jnp.where(lanes == per_row(labels_ref, logits.shape), 1.0, 0.0)
        valid = lax.broadcasted_iota(jnp.int32, logits.shape, 0) < 4
        grad_logits = jnp.where(valid, probs - onehot, 0.0).astype(BF16)
        grad_hidden = jnp.dot(grad_logits, second, preferred_element_type=F32)
        grad_pre = (grad_hidden * silu_slope(pre)).astype(BF16)
        hold[...] = jnp.zeros_like(hold)
        hold[0:8, :] = normed.astype(F32)
        hold[8:16, 0:channels] = grad_pre.astype(F32)
        hold[8:16, channels:] = hidden.astype(F32)
        hold[16:24, 0:languages] = grad_logits.astype(F32)
        lines_ref[...] = hold[...].astype(BF16)
        low = grad_pre[:, :half]
        high = grad_pre[:, half:]
        mine = jnp.where(core == 0, low, high)
        theirs = jnp.where(core == 0, high, low)
        grad_normed = lax.dot_general(mine, own_ref[...], dims, preferred_element_type=F32)
        grad_normed += lax.dot_general(theirs, other_ref[...], dims, preferred_element_type=F32)
        mean = jnp.mean(grad_normed * unit, axis=-1, keepdims=True)
        grad_pooled = r * (grad_normed - unit * mean)
        rev_ref[...] = -REVERSAL * grad_pooled / per_row(lens_ref, (8, 1)).astype(F32)


def critic_sums_kernel(band_rows, parts, sec_ref, yl_ref, core_ref, lines_ref, kept_ref, sent_ref, crit):
    n_yl, n_z, n_c = parts
    n_dp = n_yl * n_z * n_c
    features = lines_ref.shape[1]
    channels = features // 2
    padded = crit.shape[0] // n_dp
    share = channels // n_dp

    def grow(block):
        return jnp.concatenate([block, jnp.zeros_like(block)], axis=0).astype(BF16)

    def pick(shape, test):
        rows = lax.broadcasted_iota(jnp.int32, shape, 0)
        columns = lax.broadcasted_iota(jnp.int32, shape, 1)
        return jnp.where(test(rows, columns), 1.0, 0.0).astype(BF16)

    lines = lines_ref[...].astype(F32)
    base = sec_ref[0] * band_rows
    band = pick((features, 256), lambda i, j: (i == j + base) & (j < band_rows))
    nb = jnp.dot(grow(lines[0:8]), band, preferred_element_type=F32).astype(BF16)
    wide = (channels, n_dp * padded)
    columns = lax.broadcasted_iota(jnp.int32, (1, wide[1]), 1)
    slot = lax.div(columns, padded)
    inside = columns - slot * padded
    source = jnp.where(inside < share, slot * share + inside, -1)
    spread = jnp.where(lax.broadcasted_iota(jnp.int32, wide, 0) == source, 1.0, 0.0).astype(BF16)
    both = grow(lines[8:16])
    gp = jnp.dot(both[:, :channels], spread, preferred_element_type=F32).astype(BF16)
    hid = jnp.dot(both[:, channels:], spread, preferred_element_type=F32).astype(BF16)
    shift = pick((128, 256), lambda i, j: j == i + 192)
    gl = jnp.dot(grow(lines[16:24, :128]), shift, preferred_element_type=F32).astype(BF16)
    dims = (((0,), (0,)), ((), ()))
    crit[...] = lax.dot_general(gp, nb, dims, preferred_element_type=F32)
    crit[...] += lax.dot_general(hid, gl, dims, preferred_element_type=F32)

    def pack(z, _):
        for dy, dc, dest in places(parts, yl_ref, core_ref, z):
            piece = crit[pl.ds(pl.multiple_of(dest * padded, 16), padded), :].astype(BF16)
            (sent_ref if dc else kept_ref)[dy, z] = piece
        return 0

    lax.fori_loop(0, n_z, pack, 0)


def places(parts, yl_ref, core_ref, z):
    n_yl, n_z, n_c = parts
    found = []
    for dy in range(n_yl):
        for dc in range(n_c):
            yl = yl_ref[0] if dy == 0 else n_yl - 1 - yl_ref[0]
            c = core_ref[0] if dc == 0 else n_c - 1 - core_ref[0]
            found.append((dy, dc, (yl * n_z + z) * n_c + c))
    return found


def plus(left, right):
    return (left.astype(F32) + right.astype(F32)).astype(BF16)


def split_kernel(kept_ref, got_ref, own_ref, other_ref):
    own_ref[...] = plus(kept_ref[0], got_ref[0])
    if kept_ref.shape[0] > 1:
        other_ref[...] = plus(kept_ref[1], got_ref[1])


def add_kernel(left_ref, right_ref, out_ref):
    out_ref[...] = plus(left_ref[...], right_ref[...])


def pick_kernel(flag_ref, moved_ref, held_ref, out_ref):
    @pl.when(flag_ref[0] != 0)
    def _():
        out_ref[...] = moved_ref[...]

    @pl.when(flag_ref[0] == 0)
    def _():
        out_ref[...] = held_ref[...]


def finish_kernel(parts, yl_ref, core_ref, xn_ref, g_ref, h_ref, da_ref, *refs):
    outs, (down, up) = refs[:-2], refs[-2:]
    n_yl, n_z, n_c = parts
    features = xn_ref.shape[1]
    dims = (((0,), (0,)), ((), ()))
    width = 256
    for k in range(features // width):
        cols = pl.ds(k * width, width)
        down[cols, :] = lax.dot_general(xn_ref[:, cols], da_ref[...], dims, preferred_element_type=F32)
        up[cols, :] = lax.dot_general(g_ref[:, cols], h_ref[...], dims, preferred_element_type=F32)
    span = features // (n_yl * n_z * n_c)

    def pack(z, _):
        for dy, dc, dest in places(parts, yl_ref, core_ref, z):
            rows = pl.ds(pl.multiple_of(dest * span, 8), span)
            piece = jnp.concatenate([down[rows, :], up[rows, :]], axis=0)
            outs[dc * n_yl + dy][z] = piece.astype(BF16)
        return 0

    lax.fori_loop(0, n_z, pack, 0)


def join_kernel(sec_ref, *refs):
    *parts, out_ref = refs
    rows = parts[0].shape[0]

    @pl.when(sec_ref[0] % 2 == 1)
    def _():
        for i, ref in enumerate(parts):
            out_ref[i * rows : (i + 1) * rows, :] = ref[...]


def after(value, token):
    return lax.optimization_barrier((value, token))[0]


def swap(block, axis, size):
    return lax.ppermute(block, axis, [(i, size - 1 - i) for i in range(size)])


def body(parts, *args):
    return whole(parts, *args)


def whole(parts, section_in, top_grad, seq_lengths, lang_labels, norm_gain, w_down, w_up, critic_first, critic_second):
    n_yl, n_z, n_c = parts
    n_dp = n_yl * n_z * n_c
    sec = lax.axis_index(SEC)
    core = lax.axis_index("c")
    micros, seq_len, features = 4, 128, section_in.shape[-1]
    rank = w_down.shape[-1]
    rows = micros * seq_len
    chunks = rows // CHUNK
    x = section_in.reshape(rows, features)
    top = top_grad.reshape(rows, features)
    gain = norm_gain.reshape(1, features)
    wd = w_down[0]
    sec_s = sec.reshape(1).astype(jnp.int32)
    core_s = core.reshape(1).astype(jnp.int32)
    channels = critic_first.shape[1]
    half = channels // 2
    sds = jax.ShapeDtypeStruct

    lens = seq_lengths.reshape(micros)
    mine = call(
        half_kernel,
        sds((critic_first.shape[0], half), BF16),
        [SM, HB],
        (core_s, critic_first),
        0,
        1 << 19,
        scratch=[pltpu.SemaphoreType.DMA], limit=16,
    )
    even = lax.ppermute(mine, SEC, [(i, i + 1) for i in range(0, SECTIONS, 2)])
    languages = critic_second.shape[1]
    x, top, gain_v, second, xn, h, a, q, pooled, wut, wdt, grads, inner = call(
        prepare_kernel,
        (
            sds((rows, features), BF16),
            sds((rows, features), BF16),
            sds((1, features), F32),
            sds((languages, channels), BF16),
            sds((rows, features), BF16),
            sds((rows, rank), BF16),
            sds((rows, rank), F32),
            sds((rows, 128), F32),
            sds((8, features), F32),
            sds((features, rank), BF16),
            sds((rank, features), BF16),
            sds((rows, features), BF16),
            sds((rows, rank), BF16),
        ),
        [SM] + [HB] * 6,
        (lens, x, top, gain, critic_second.T, wd, w_up[0]),
        2 * rows * features * rank,
        8 << 20,
        scratch=[pltpu.VMEM((features, rank), BF16), pltpu.VMEM((rank, features), BF16), pltpu.SemaphoreType.DMA((9,))], limit=16,
    )

    three = SECTIONS // 2 - 1
    held = {}
    yl_s = lax.axis_index("yl").reshape(1).astype(jnp.int32)
    band_rows = critic_first.shape[0]
    share = channels // n_dp
    padded = -(-share // 16) * 16

    def join(token, *pieces):
        return call(
            join_kernel,
            sds((len(pieces) * pieces[0].shape[0], half), BF16),
            [SM] + [VM] * len(pieces),
            (after(sec_s, token), *pieces),
            0,
            2 << 20,
        )

    def side_work(step, token):
        if step == 0:
            held["pair"] = join(token, even, mine)
            held["far"] = [lax.ppermute(held["pair"], SEC, [(i, three)]) for i in (7, 5, 1)]
        elif step == 1:
            held["pooled"] = lax.ppermute(after(pooled, token), SEC, [(4, three)])
        elif step == 4:
            far = held["far"]
            held["own"] = join(token, far[2], held["pair"], far[1], far[0])
            pairs = [(three * 2, three * 2 + 1), (three * 2 + 1, three * 2)]
            held["other"] = lax.ppermute(held["own"], SEC + ("c",), pairs)
        elif step == 7:
            held["lines"], held["rev"] = call(
                critic_kernel,
                (sds((32, features), BF16), sds((8, features), F32)),
                [SM] * 4 + [VM] * 4,
                (
                    after(sec_s, token),
                    core_s,
                    lang_labels.reshape(micros),
                    lens,
                    held["pooled"],
                    held["own"],
                    held["other"],
                    second,
                ),
                1 << 27,
                4 << 20,
                scratch=[pltpu.VMEM((32, features), F32)],
            )
        elif step in (8, 10, 12):
            lines = after(held["lines"], token)
            if step == 8:
                route, gets = [(3, 7)], sec == 7
            elif step == 10:
                route, gets = [(3, 1), (7, 5)], (sec == 1) | (sec == 5)
            else:
                route, gets = [(i + 1, i) for i in range(0, SECTIONS, 2)], sec % 2 == 0
            moved = lax.ppermute(lines, SEC, route)
            held["moved"] = (gets.astype(jnp.int32).reshape(1), moved)
        elif step == 14:
            kept, sent = call(
                functools.partial(critic_sums_kernel, band_rows, parts),
                (sds((n_yl, n_z, padded, rank), BF16),) * 2,
                [SM, SM, SM, VM],
                (after(sec_s, token), yl_s, core_s, held["lines"]),
                1 << 26,
                1 << 20,
                scratch=[pltpu.VMEM((n_dp * padded, rank), F32)],
            )
            held["kept"] = kept
            held["got"] = swap(sent, "c", n_c)
        elif step == 16:
            one = sds((n_z, padded, rank), BF16)
            own, other = call(split_kernel, (one, one), [VM, VM], (after(held["kept"], token), held["got"]), 0, 1 << 20)
            held["own_sum"] = own
            if n_yl == 2:
                held["other_sum"] = swap(other, "yl", n_yl)
        elif step == 19 and n_yl == 2:
            args = (after(held["own_sum"], token), held["other_sum"])
            held["own_sum"] = call(add_kernel, sds(args[0].shape, BF16), [VM, VM], args, 0, 1 << 20)
        if step in (9, 11, 13):
            flag, moved = held.pop("moved")
            held["lines"] = call(
                pick_kernel,
                sds(held["lines"].shape, BF16),
                [SM, VM, VM],
                (after(flag, token), moved, held["lines"]),
                0,
                1 << 18,
            )

    steps = DELAY * (SECTIONS - 1) + chunks
    received = {}
    route = [(i, i - 1) for i in range(1, SECTIONS)]
    for step in range(steps):
        has_top = step < chunks
        has_in = step >= DELAY
        first_rev = DELAY * (SECTIONS - 1 - three)
        has_rev = first_rev <= step < first_rev + chunks
        args = [sec_s, lens, x, a, q, gain_v, wut, wdt]
        specs = [SM, SM] + [VM] * 6
        if has_top:
            args.append(top)
        if has_in:
            args.append(received.pop(step - DELAY))
        if has_rev:
            args.append(held["rev"])
        args += [grads, inner]
        specs += [VM] * (len(args) - len(specs))
        outgoing, grads, inner = call(
            functools.partial(step_kernel, step, chunks, has_top, has_in, has_rev),
            (sds((CHUNK, features), BF16), sds((rows, features), BF16), sds((rows, rank), BF16)),
            specs,
            tuple(args),
            4 * CHUNK * features * rank,
            3 << 20,
            aliases={len(args) - 2: 1, len(args) - 1: 2},
        )
        if step < steps - DELAY:
            received[step] = lax.ppermute(outgoing, SEC, route)
        side_work(step, outgoing)

    span = features // n_dp
    piece = sds((n_z, 2 * span, rank), BF16)
    packed = call(
        functools.partial(finish_kernel, parts),
        (piece,) * (n_yl * n_c),
        [SM, SM] + [VM] * 4,
        (yl_s, core_s, xn, grads, h, inner),
        4 * rows * features * rank,
        8 << 20,
        scratch=[pltpu.VMEM((features, rank), F32)] * 2,
    )

    kept, sent = packed[:n_yl], packed[n_yl:]
    halves = [None] * n_yl
    for i in reversed(range(n_yl)):
        halves[i] = plus(kept[i], swap(sent[i], "c", n_c))
    summed = halves[0]
    crit = after(held["own_sum"], summed)
    if n_z > 1:
        crit = lax.all_to_all(crit, "z", 0, 0, tiled=True)
    if n_yl == 2:
        moved = swap(halves[1], "yl", n_yl)
        summed = plus(summed, after(moved, crit))
    if n_z > 1:
        summed = lax.all_to_all(summed, "z", 0, 0, tiled=True)
    total = jnp.sum(summed.astype(F32), axis=0)
    down = total[:span]
    up = total[span:].T
    crit = jnp.sum(crit.astype(F32), axis=0)[:share]
    dp_place = lax.axis_index(("yl", "z", "c"))
    wd_own = lax.dynamic_slice_in_dim(wd, dp_place * span, span, 0).astype(F32)
    gain_own = lax.dynamic_slice_in_dim(gain[0], dp_place * span, span, 0)
    grad_gain = jnp.sum(down * wd_own, axis=1) / gain_own
    first = crit[:, :band_rows].T
    second_grad = crit[:, 192 : 192 + critic_second.shape[1]]
    return (down[None], up[None], grad_gain[None], first, second_grad)


def solution(mesh):
    n_dp = mesh.shape["dp"]
    parts = (2, n_dp // 4, 2) if n_dp >= 8 else (1, n_dp // 2, 2)
    fine = Mesh(mesh.devices.reshape((SECTIONS // 2, 2) + parts), SEC + ("yl", "z", "c"))
    dp = ("yl", "z", "c")
    return jax.shard_map(
        functools.partial(body, parts),
        mesh=fine,
        in_specs=(
            P(SEC, None, dp, None, None),
            P(None, dp, None, None),
            P(None, dp),
            P(None, dp),
            P(SEC, None),
            P(SEC, None, None),
            P(SEC, None, None),
            P(SEC, None),
            P(),
        ),
        out_specs=(P(SEC, dp, None), P(SEC, None, dp), P(SEC, dp), P(SEC, dp), P(dp, None)),
        check_vma=False,
    )
```

```python
import functools

import jax
import jax.numpy as jnp
from jax import lax
from jax.experimental import pallas as pl
from jax.experimental.pallas import tpu as pltpu
from jax.sharding import Mesh, PartitionSpec as P


EPSILON = 1e-06
REVERSAL = 0.5
SECTIONS = 8
CHUNK = 64
STAY = [2, 3, 4, 6, 7]
DELAY = 2
SEC = ("x", "yh")
F32 = jnp.float32
BF16 = jnp.bfloat16
VM = pl.BlockSpec(memory_space=pltpu.VMEM)
SM = pl.BlockSpec(memory_space=pltpu.SMEM)


def silu_slope(pre_act):
    sigma = jax.nn.sigmoid(pre_act)
    return sigma * (1.0 + pre_act * (1.0 - sigma))


def call(kernel, out_shape, in_specs, args, flops, moved, aliases=None, scratch=(), limit=16):
    return pl.pallas_call(
        kernel,
        out_shape=out_shape,
        in_specs=in_specs,
        out_specs=jax.tree.map(lambda _: VM, out_shape),
        input_output_aliases=aliases or {},
        scratch_shapes=scratch,
        compiler_params=pltpu.CompilerParams(vmem_limit_bytes=limit << 20),
        cost_estimate=pl.CostEstimate(flops=flops, bytes_accessed=moved, transcendentals=0),
    )(*args)


def half_kernel(core_ref, first_ref, mine_ref):
    half = mine_ref.shape[1]
    for c in range(2):

        @pl.when(core_ref[0] == c)
        def _():
            mine_ref[...] = first_ref[:, c * half : (c + 1) * half]


def prepare_kernel(lens_ref, _yl, x_ref, gain_ref, wd_ref, wu_ref, *refs):
    xn_ref, h_ref, a_ref, q_ref, pooled_ref, wut_ref, wdt_ref, _, _ = refs
    micros, seq_len = 4, 128
    gain = gain_ref[0:1, :]
    wut_ref[...] = wu_ref[...].T
    wdt_ref[...] = wd_ref[...].T
    pooled_ref[...] = jnp.zeros_like(pooled_ref)
    positions = lax.broadcasted_iota(jnp.int32, (seq_len, 1), 0)
    for m in range(micros):
        rows = pl.ds(m * seq_len, seq_len)
        values = x_ref[rows, :].astype(F32)
        count = lens_ref[m]
        total = jnp.sum(jnp.where(positions < count, values, 0.0), axis=0, keepdims=True)
        pooled_ref[m : m + 1, :] = total / count.astype(F32)
        q = lax.rsqrt(jnp.mean(values * values, axis=-1, keepdims=True) + EPSILON)
        normed = (values * q * gain).astype(BF16)
        xn_ref[rows, :] = normed
        a = jnp.dot(normed, wd_ref[...], preferred_element_type=F32)
        a_ref[rows, :] = a
        h_ref[rows, :] = (a * jax.nn.sigmoid(a)).astype(BF16)
        q_ref[rows, :] = jnp.broadcast_to(q, (seq_len, 128))


def step_kernel(step, chunks, has_top, has_in, has_rev, *refs):
    refs = list(refs)
    sec_ref, lens_ref, x_ref, a_ref, q_ref, gain_ref, wut_ref, wdt_ref = refs[:8]
    refs = refs[8:]
    top_ref = refs.pop(0) if has_top else None
    in_ref = refs.pop(0) if has_in else None
    rev_ref = refs.pop(0) if has_rev else None
    out_ref, g_ref, da_ref = refs[2:5]
    features = x_ref.shape[1]
    sec = sec_ref[0]
    place = step - DELAY * (SECTIONS - 1 - sec)
    live = (place >= 0) & (place < chunks)
    place = jnp.clip(place, 0, chunks - 1)
    rows = pl.ds(pl.multiple_of(place * CHUNK, CHUNK), CHUNK)

    if has_top:

        @pl.when(live & (sec == SECTIONS - 1))
        def _():
            g_ref[rows, :] = top_ref[rows, :]

    if has_in:

        @pl.when(live & (sec < SECTIONS - 1))
        def _():
            g_ref[rows, :] = in_ref[...]

    if has_rev:

        @pl.when(live & (sec == SECTIONS // 2 - 1))
        def _():
            per = 128 // CHUNK
            micro = lax.div(place, per)
            first = lax.rem(place, per) * CHUNK
            positions = lax.broadcasted_iota(jnp.int32, (CHUNK, 1), 0) + first
            extra = jnp.where(positions < lens_ref[micro], rev_ref[pl.ds(micro, 1), :], 0.0)
            g_ref[rows, :] = (in_ref[...].astype(F32) + extra).astype(BF16)

    @pl.when(live)
    def _():
        g = g_ref[rows, :]
        a = a_ref[rows, :]
        q = q_ref[rows, 0:1]
        dh = jnp.dot(g, wut_ref[...], preferred_element_type=F32)
        da = (dh * silu_slope(a)).astype(BF16)
        da_ref[rows, :] = da
        mean = jnp.sum(da.astype(F32) * a, axis=-1, keepdims=True) * (1.0 / features)
        dxn = jnp.dot(da, wdt_ref[...], preferred_element_type=F32)
        x = x_ref[rows, :].astype(F32)
        out = g.astype(F32) + q * (dxn * gain_ref[0:1, :]) - x * (q * q * mean)
        out_ref[...] = out.astype(BF16)


def per_row(ref, shape):
    rows = lax.broadcasted_iota(jnp.int32, shape, 0)
    column = jnp.ones(shape, jnp.int32)
    for m in range(4):
        column = jnp.where(rows == m, ref[m], column)
    return column


def critic_kernel(
    sec_ref, core_ref, labels_ref, lens_ref, pooled_ref, own_ref, other_ref, second_ref, lines_ref, rev_ref, hold
):
    half = own_ref.shape[1]
    channels = 2 * half
    languages = second_ref.shape[0]

    @pl.when(sec_ref[0] == SECTIONS // 2 - 1)
    def _():
        pooled = pooled_ref[...].astype(BF16).astype(F32)
        r = lax.rsqrt(jnp.mean(pooled * pooled, axis=-1, keepdims=True) + EPSILON)
        unit = pooled * r
        normed = unit.astype(BF16)
        core = core_ref[0]
        pre_own = jnp.dot(normed, own_ref[...], preferred_element_type=F32)
        pre_other = jnp.dot(normed, other_ref[...], preferred_element_type=F32)
        low = jnp.where(core == 0, pre_own, pre_other)
        high = jnp.where(core == 0, pre_other, pre_own)
        pre = jnp.concatenate([low, high], axis=1)
        hidden = (pre * jax.nn.sigmoid(pre)).astype(BF16)
        second = second_ref[...]
        dims = (((1,), (1,)), ((), ()))
        logits = lax.dot_general(hidden, second, dims, preferred_element_type=F32)
        exponent = jnp.exp(logits)
        probs = exponent / jnp.sum(exponent, axis=-1, keepdims=True)
        lanes = lax.broadcasted_iota(jnp.int32, logits.shape, 1)
        onehot = jnp.where(lanes == per_row(labels_ref, logits.shape), 1.0, 0.0)
        valid = lax.broadcasted_iota(jnp.int32, logits.shape, 0) < 4
        grad_logits = jnp.where(valid, probs - onehot, 0.0).astype(BF16)
        grad_hidden = jnp.dot(grad_logits, second, preferred_element_type=F32)
        grad_pre = (grad_hidden * silu_slope(pre)).astype(BF16)
        hold[...] = jnp.zeros_like(hold)
        hold[0:8, :] = normed.astype(F32)
        hold[8:16, 0:channels] = grad_pre.astype(F32)
        hold[8:16, channels:] = hidden.astype(F32)
        hold[16:24, 0:languages] = grad_logits.astype(F32)
        lines_ref[...] = hold[...].astype(BF16)
        low = grad_pre[:, :half]
        high = grad_pre[:, half:]
        mine = jnp.where(core == 0, low, high)
        theirs = jnp.where(core == 0, high, low)
        grad_normed = lax.dot_general(mine, own_ref[...], dims, preferred_element_type=F32)
        grad_normed += lax.dot_general(theirs, other_ref[...], dims, preferred_element_type=F32)
        mean = jnp.mean(grad_normed * unit, axis=-1, keepdims=True)
        grad_pooled = r * (grad_normed - unit * mean)
        rev_ref[...] = -REVERSAL * grad_pooled / per_row(lens_ref, (8, 1)).astype(F32)


def critic_sums_kernel(band_rows, parts, sec_ref, yl_ref, core_ref, lines_ref, kept_ref, sent_ref, crit):
    n_yl, n_z, n_c = parts
    n_dp = n_yl * n_z * n_c
    features = lines_ref.shape[1]
    channels = features // 2
    padded = crit.shape[0] // n_dp
    share = channels // n_dp

    def grow(block):
        return jnp.concatenate([block, jnp.zeros_like(block)], axis=0).astype(BF16)

    def pick(shape, test):
        rows = lax.broadcasted_iota(jnp.int32, shape, 0)
        columns = lax.broadcasted_iota(jnp.int32, shape, 1)
        return jnp.where(test(rows, columns), 1.0, 0.0).astype(BF16)

    lines = lines_ref[...].astype(F32)
    base = sec_ref[0] * band_rows
    band = pick((features, 256), lambda i, j: (i == j + base) & (j < band_rows))
    nb = jnp.dot(grow(lines[0:8]), band, preferred_element_type=F32).astype(BF16)
    wide = (channels, n_dp * padded)
    columns = lax.broadcasted_iota(jnp.int32, (1, wide[1]), 1)
    slot = lax.div(columns, padded)
    inside = columns - slot * padded
    source = jnp.where(inside < share, slot * share + inside, -1)
    spread = jnp.where(lax.broadcasted_iota(jnp.int32, wide, 0) == source, 1.0, 0.0).astype(BF16)
    both = grow(lines[8:16])
    gp = jnp.dot(both[:, :channels], spread, preferred_element_type=F32).astype(BF16)
    hid = jnp.dot(both[:, channels:], spread, preferred_element_type=F32).astype(BF16)
    shift = pick((128, 256), lambda i, j: j == i + 192)
    gl = jnp.dot(grow(lines[16:24, :128]), shift, preferred_element_type=F32).astype(BF16)
    dims = (((0,), (0,)), ((), ()))
    crit[...] = lax.dot_general(gp, nb, dims, preferred_element_type=F32)
    crit[...] += lax.dot_general(hid, gl, dims, preferred_element_type=F32)

    def pack(z, _):
        for dy, dc, dest in places(parts, yl_ref, core_ref, z):
            piece = crit[pl.ds(pl.multiple_of(dest * padded, 16), padded), :].astype(BF16)
            (sent_ref if dc else kept_ref)[dy, z] = piece
        return 0

    lax.fori_loop(0, n_z, pack, 0)


def places(parts, yl_ref, core_ref, z):
    n_yl, n_z, n_c = parts
    found = []
    for dy in range(n_yl):
        for dc in range(n_c):
            yl = yl_ref[0] if dy == 0 else n_yl - 1 - yl_ref[0]
            c = core_ref[0] if dc == 0 else n_c - 1 - core_ref[0]
            found.append((dy, dc, (yl * n_z + z) * n_c + c))
    return found


def plus(left, right):
    return (left.astype(F32) + right.astype(F32)).astype(BF16)


def split_kernel(kept_ref, got_ref, own_ref, other_ref):
    own_ref[...] = plus(kept_ref[0], got_ref[0])
    if kept_ref.shape[0] > 1:
        other_ref[...] = plus(kept_ref[1], got_ref[1])


def copy_kernel(source_ref, out_ref):
    out_ref[...] = source_ref[...]


def add_kernel(left_ref, right_ref, out_ref):
    out_ref[...] = plus(left_ref[...], right_ref[...])


def pick_kernel(targets, sec_ref, moved_ref, held_ref, out_ref):
    gets = functools.reduce(jnp.logical_or, [sec_ref[0] == target for target in targets])

    @pl.when(gets)
    def _():
        out_ref[...] = moved_ref[...]

    @pl.when(jnp.logical_not(gets))
    def _():
        out_ref[...] = held_ref[...]


def finish_kernel(parts, yl_ref, core_ref, xn_ref, g_ref, h_ref, da_ref, *refs):
    outs, (down, up) = refs[:-2], refs[-2:]
    n_yl, n_z, n_c = parts
    features = xn_ref.shape[1]
    dims = (((0,), (0,)), ((), ()))
    width = 256
    for k in range(features // width):
        cols = pl.ds(k * width, width)
        down[cols, :] = lax.dot_general(xn_ref[:, cols], da_ref[...], dims, preferred_element_type=F32)
        up[cols, :] = lax.dot_general(g_ref[:, cols], h_ref[...], dims, preferred_element_type=F32)
    span = features // (n_yl * n_z * n_c)

    def pack(z, _):
        for dy, dc, dest in places(parts, yl_ref, core_ref, z):
            rows = pl.ds(pl.multiple_of(dest * span, 8), span)
            piece = jnp.concatenate([down[rows, :], up[rows, :]], axis=0)
            outs[dc * n_yl + dy][z] = piece.astype(BF16)
        return 0

    lax.fori_loop(0, n_z, pack, 0)


def join_kernel(sec_ref, *refs):
    *parts, out_ref = refs
    rows = parts[0].shape[0]

    @pl.when(sec_ref[0] % 2 == 1)
    def _():
        for i, ref in enumerate(parts):
            out_ref[i * rows : (i + 1) * rows, :] = ref[...]


def after(value, token):
    return lax.optimization_barrier((value, token))[0]


def swap(block, axis, size):
    return lax.ppermute(block, axis, [(i, size - 1 - i) for i in range(size)])


def body(parts, *args):
    return whole(parts, *args)


def whole(parts, section_in, top_grad, seq_lengths, lang_labels, norm_gain, w_down, w_up, critic_first, critic_second):
    n_yl, n_z, n_c = parts
    n_dp = n_yl * n_z * n_c
    sec = lax.axis_index(SEC)
    core = lax.axis_index("c")
    micros, seq_len, features = 4, 128, section_in.shape[-1]
    rank = w_down.shape[-1]
    rows = micros * seq_len
    chunks = rows // CHUNK
    x = section_in.reshape(rows, features)
    top = top_grad.reshape(rows, features)
    gain = norm_gain.reshape(1, features)
    wd = w_down[0]
    sec_s = sec.reshape(1).astype(jnp.int32)
    core_s = core.reshape(1).astype(jnp.int32)
    yl_s = lax.axis_index("yl").reshape(1).astype(jnp.int32)
    channels = critic_first.shape[1]
    half = channels // 2
    sds = jax.ShapeDtypeStruct

    lens = seq_lengths.reshape(micros)
    mine = call(
        half_kernel,
        sds((critic_first.shape[0], half), BF16),
        [SM, VM],
        (core_s, critic_first),
        0,
        1 << 19,
    )
    even = lax.ppermute(mine, SEC, [(i, i + 1) for i in range(0, SECTIONS, 2)])
    second = critic_second.T
    xn, h, a, q, pooled, wut, wdt, grads, inner = call(
        prepare_kernel,
        (
            sds((rows, features), BF16),
            sds((rows, rank), BF16),
            sds((rows, rank), F32),
            sds((rows, 128), F32),
            sds((8, features), F32),
            sds((features, rank), BF16),
            sds((rank, features), BF16),
            sds((rows, features), BF16),
            sds((rows, rank), BF16),
        ),
        [SM, SM] + [VM] * 4,
        (lens, yl_s, x, gain, wd, w_up[0]),
        2 * rows * features * rank,
        8 << 20,
    )

    three = SECTIONS // 2 - 1
    held = {}
    band_rows = critic_first.shape[0]
    share = channels // n_dp
    padded = -(-share // 16) * 16

    def join(token, *pieces):
        return call(
            join_kernel,
            sds((len(pieces) * pieces[0].shape[0], half), BF16),
            [SM] + [VM] * len(pieces),
            (after(sec_s, token), *pieces),
            0,
            2 << 20,
        )

    def side_work(step, token):
        if step == 0:
            held["pair"] = join(token, even, mine)
            held["far"] = [lax.ppermute(held["pair"], SEC, [(i, three)]) for i in (7, 5, 1)]
        elif step == 1:
            held["pooled"] = lax.ppermute(after(pooled, token), SEC, [(4, three)])
        elif step == 4:
            far = held["far"]
            held["own"] = join(token, far[2], held["pair"], far[1], far[0])
            pairs = [(three * 2, three * 2 + 1), (three * 2 + 1, three * 2)]
            held["other"] = lax.ppermute(held["own"], SEC + ("c",), pairs)
        elif step == 7:
            held["lines"], held["rev"] = call(
                critic_kernel,
                (sds((32, features), BF16), sds((8, features), F32)),
                [SM] * 4 + [VM] * 4,
                (
                    after(sec_s, token),
                    core_s,
                    lang_labels.reshape(micros),
                    lens,
                    held["pooled"],
                    held["own"],
                    held["other"],
                    second,
                ),
                1 << 27,
                4 << 20,
                scratch=[pltpu.VMEM((32, features), F32)],
            )
        elif step in (8, 10, 12):
            lines = after(held["lines"], token)
            if step == 8:
                route = [(3, 7)]
            elif step == 10:
                route = [(3, 1), (7, 5)]
            else:
                route = [(i + 1, i) for i in range(0, SECTIONS, 2)]
            moved = lax.ppermute(lines, SEC, route)
            held["moved"] = ([target for _, target in route], moved)
        elif step == 14:
            kept, sent = call(
                functools.partial(critic_sums_kernel, band_rows, parts),
                (sds((n_yl, n_z, padded, rank), BF16),) * 2,
                [SM, SM, SM, VM],
                (after(sec_s, token), yl_s, core_s, held["lines"]),
                1 << 26,
                1 << 20,
                scratch=[pltpu.VMEM((n_dp * padded, rank), F32)],
            )
            held["kept"] = kept
            held["got"] = swap(sent, "c", n_c)
        elif step == 16:
            one = sds((n_z, padded, rank), BF16)
            own, other = call(
                split_kernel, (one, one), [VM, VM], (after(held["kept"], token), held["got"]), 0, 1 << 20
            )
            held["own_sum"] = own
            if n_yl == 2:
                held["other_sum"] = swap(other, "yl", n_yl)
        elif step == 19 and n_yl == 2:
            args = (after(held["own_sum"], token), held["other_sum"])
            held["own_sum"] = call(add_kernel, sds(args[0].shape, BF16), [VM, VM], args, 0, 1 << 20)
        if step in (9, 11, 13):
            targets, moved = held.pop("moved")
            held["lines"] = call(
                functools.partial(pick_kernel, targets),
                sds(held["lines"].shape, BF16),
                [SM, VM, VM],
                (after(sec_s, token), moved, held["lines"]),
                0,
                1 << 18,
            )

    steps = DELAY * (SECTIONS - 1) + chunks
    received = {}
    relay_route = [(i, i - 1) for i in range(1, SECTIONS)]
    for step in range(steps):
        has_top = step < chunks
        has_in = step >= DELAY
        first_rev = DELAY * (SECTIONS - 1 - three)
        has_rev = first_rev <= step < first_rev + chunks
        args = [sec_s, lens, x, a, q, gain, wut, wdt]
        specs = [SM, SM] + [VM] * 6
        if has_top:
            args.append(top)
        if has_in:
            args.append(received.pop(step - DELAY))
        if has_rev:
            args.append(held["rev"])
        args += [grads, inner]
        specs += [VM] * (len(args) - len(specs))
        passed = [len(args) - 2, len(args) - 1] + STAY
        outgoing, grads, inner, *stay = call(
            functools.partial(step_kernel, step, chunks, has_top, has_in, has_rev),
            (sds((CHUNK, features), BF16),) + tuple(sds(args[i].shape, args[i].dtype) for i in passed),
            specs,
            tuple(args),
            4 * CHUNK * features * rank,
            3 << 20,
            aliases={i: k + 1 for k, i in enumerate(passed)},
        )
        x, a, q, wut, wdt = stay
        if step < steps - DELAY:
            received[step] = lax.ppermute(outgoing, SEC, relay_route)
        side_work(step, outgoing)

    span = features // n_dp
    piece = sds((n_z, 2 * span, rank), BF16)
    packed = call(
        functools.partial(finish_kernel, parts),
        (piece,) * (n_yl * n_c),
        [SM, SM] + [VM] * 4,
        (yl_s, core_s, xn, grads, h, inner),
        4 * rows * features * rank,
        8 << 20,
        scratch=[pltpu.VMEM((features, rank), F32)] * 2,
    )

    kept, sent = packed[:n_yl], packed[n_yl:]
    halves = [None] * n_yl
    for i in reversed(range(n_yl)):
        halves[i] = plus(kept[i], swap(sent[i], "c", n_c))
    summed = halves[0]
    crit = held["own_sum"]
    if n_yl == 2:
        moved = swap(halves[1], "yl", n_yl)
        crit = call(copy_kernel, sds(crit.shape, BF16), [VM], (after(crit, halves[1]),), 0, 1 << 18)
    if n_z > 1:
        crit = lax.all_to_all(crit, "z", 0, 0, tiled=True)
    if n_yl == 2:
        summed = plus(summed, after(moved, crit))
    if n_z > 1:
        summed = lax.all_to_all(summed, "z", 0, 0, tiled=True)
    total = jnp.sum(summed.astype(F32), axis=0)
    down = total[:span]
    up = total[span:].T
    crit = jnp.sum(crit.astype(F32), axis=0)[:share]
    dp_place = lax.axis_index(("yl", "z", "c"))
    wd_own = lax.dynamic_slice_in_dim(wd, dp_place * span, span, 0).astype(F32)
    gain_own = lax.dynamic_slice_in_dim(gain[0], dp_place * span, span, 0)
    grad_gain = jnp.sum(down * wd_own, axis=1) / gain_own
    first = crit[:, :band_rows].T
    second_grad = crit[:, 192 : 192 + critic_second.shape[1]]
    return (down[None], up[None], grad_gain[None], first, second_grad)


def solution(mesh):
    n_dp = mesh.shape["dp"]
    parts = (2, n_dp // 4, 2) if n_dp >= 8 else (1, n_dp // 2, 2)
    fine = Mesh(mesh.devices.reshape((SECTIONS // 2, 2) + parts), SEC + ("yl", "z", "c"))
    dp = ("yl", "z", "c")
    return jax.shard_map(
        functools.partial(body, parts),
        mesh=fine,
        in_specs=(
            P(SEC, None, dp, None, None),
            P(None, dp, None, None),
            P(None, dp),
            P(None, dp),
            P(SEC, None),
            P(SEC, None, None),
            P(SEC, None, None),
            P(SEC, None),
            P(),
        ),
        out_specs=(P(SEC, dp, None), P(SEC, None, dp), P(SEC, dp), P(SEC, dp), P(dp, None)),
        check_vma=False,
    )
```

```python
import functools

import jax
import jax.numpy as jnp
from jax import lax
from jax.experimental import pallas as pl
from jax.experimental.pallas import tpu as pltpu
from jax.sharding import Mesh, PartitionSpec as P


EPSILON = 1e-06
REVERSAL = 0.5
SECTIONS = 8
CHUNK = 64
STAY = [2, 3, 4, 6, 7]
DELAY = 2
SEC = ("x", "yh")
F32 = jnp.float32
BF16 = jnp.bfloat16
VM = pl.BlockSpec(memory_space=pltpu.VMEM)
SM = pl.BlockSpec(memory_space=pltpu.SMEM)


def silu_slope(pre_act):
    sigma = jax.nn.sigmoid(pre_act)
    return sigma * (1.0 + pre_act * (1.0 - sigma))


def call(kernel, out_shape, in_specs, args, flops, moved, aliases=None, scratch=(), limit=16):
    return pl.pallas_call(
        kernel,
        out_shape=out_shape,
        in_specs=in_specs,
        out_specs=jax.tree.map(lambda _: VM, out_shape),
        input_output_aliases=aliases or {},
        scratch_shapes=scratch,
        compiler_params=pltpu.CompilerParams(vmem_limit_bytes=limit << 20),
        cost_estimate=pl.CostEstimate(flops=flops, bytes_accessed=moved, transcendentals=0),
    )(*args)


def half_kernel(core_ref, first_ref, mine_ref):
    half = mine_ref.shape[1]
    for c in range(2):

        @pl.when(core_ref[0] == c)
        def _():
            mine_ref[...] = first_ref[:, c * half : (c + 1) * half]


def prepare_kernel(lens_ref, _yl, x_ref, gain_ref, wd_ref, wu_ref, *refs):
    xn_ref, h_ref, a_ref, q_ref, pooled_ref, wut_ref, wdt_ref, _, _ = refs
    micros, seq_len = 4, 128
    gain = gain_ref[0:1, :]
    wut_ref[...] = wu_ref[...].T
    wdt_ref[...] = wd_ref[...].T
    pooled_ref[...] = jnp.zeros_like(pooled_ref)
    positions = lax.broadcasted_iota(jnp.int32, (seq_len, 1), 0)
    for m in range(micros):
        rows = pl.ds(m * seq_len, seq_len)
        values = x_ref[rows, :].astype(F32)
        count = lens_ref[m]
        total = jnp.sum(jnp.where(positions < count, values, 0.0), axis=0, keepdims=True)
        pooled_ref[m : m + 1, :] = total / count.astype(F32)
        q = lax.rsqrt(jnp.mean(values * values, axis=-1, keepdims=True) + EPSILON)
        normed = (values * q * gain).astype(BF16)
        xn_ref[rows, :] = normed
        a = jnp.dot(normed, wd_ref[...], preferred_element_type=F32)
        a_ref[rows, :] = a
        h_ref[rows, :] = (a * jax.nn.sigmoid(a)).astype(BF16)
        q_ref[rows, :] = jnp.broadcast_to(q, (seq_len, 128))


def step_kernel(step, chunks, has_top, has_in, has_rev, *refs):
    refs = list(refs)
    sec_ref, lens_ref, x_ref, a_ref, q_ref, gain_ref, wut_ref, wdt_ref = refs[:8]
    refs = refs[8:]
    top_ref = refs.pop(0) if has_top else None
    in_ref = refs.pop(0) if has_in else None
    rev_ref = refs.pop(0) if has_rev else None
    out_ref, g_ref, da_ref = refs[2:5]
    features = x_ref.shape[1]
    sec = sec_ref[0]
    place = step - DELAY * (SECTIONS - 1 - sec)
    live = (place >= 0) & (place < chunks)
    place = jnp.clip(place, 0, chunks - 1)
    rows = pl.ds(pl.multiple_of(place * CHUNK, CHUNK), CHUNK)

    if has_top:

        @pl.when(live & (sec == SECTIONS - 1))
        def _():
            g_ref[rows, :] = top_ref[rows, :]

    if has_in:

        @pl.when(live & (sec < SECTIONS - 1))
        def _():
            g_ref[rows, :] = in_ref[...]

    if has_rev:

        @pl.when(live & (sec == SECTIONS // 2 - 1))
        def _():
            per = 128 // CHUNK
            micro = lax.div(place, per)
            first = lax.rem(place, per) * CHUNK
            positions = lax.broadcasted_iota(jnp.int32, (CHUNK, 1), 0) + first
            extra = jnp.where(positions < lens_ref[micro], rev_ref[pl.ds(micro, 1), :], 0.0)
            g_ref[rows, :] = (in_ref[...].astype(F32) + extra).astype(BF16)

    @pl.when(live)
    def _():
        g = g_ref[rows, :]
        a = a_ref[rows, :]
        q = q_ref[rows, 0:1]
        dh = jnp.dot(g, wut_ref[...], preferred_element_type=F32)
        da = (dh * silu_slope(a)).astype(BF16)
        da_ref[rows, :] = da
        mean = jnp.sum(da.astype(F32) * a, axis=-1, keepdims=True) * (1.0 / features)
        dxn = jnp.dot(da, wdt_ref[...], preferred_element_type=F32)
        x = x_ref[rows, :].astype(F32)
        out = g.astype(F32) + q * (dxn * gain_ref[0:1, :]) - x * (q * q * mean)
        out_ref[...] = out.astype(BF16)


def per_row(ref, shape):
    rows = lax.broadcasted_iota(jnp.int32, shape, 0)
    column = jnp.ones(shape, jnp.int32)
    for m in range(4):
        column = jnp.where(rows == m, ref[m], column)
    return column


def critic_kernel(
    sec_ref, core_ref, labels_ref, lens_ref, pooled_ref, own_ref, other_ref, second_ref, lines_ref, rev_ref, hold
):
    half = own_ref.shape[1]
    channels = 2 * half
    languages = second_ref.shape[0]

    @pl.when(sec_ref[0] == SECTIONS // 2 - 1)
    def _():
        pooled = pooled_ref[...].astype(BF16).astype(F32)
        r = lax.rsqrt(jnp.mean(pooled * pooled, axis=-1, keepdims=True) + EPSILON)
        unit = pooled * r
        normed = unit.astype(BF16)
        core = core_ref[0]
        pre_own = jnp.dot(normed, own_ref[...], preferred_element_type=F32)
        pre_other = jnp.dot(normed, other_ref[...], preferred_element_type=F32)
        low = jnp.where(core == 0, pre_own, pre_other)
        high = jnp.where(core == 0, pre_other, pre_own)
        pre = jnp.concatenate([low, high], axis=1)
        hidden = (pre * jax.nn.sigmoid(pre)).astype(BF16)
        second = second_ref[...]
        dims = (((1,), (1,)), ((), ()))
        logits = lax.dot_general(hidden, second, dims, preferred_element_type=F32)
        exponent = jnp.exp(logits)
        probs = exponent / jnp.sum(exponent, axis=-1, keepdims=True)
        lanes = lax.broadcasted_iota(jnp.int32, logits.shape, 1)
        onehot = jnp.where(lanes == per_row(labels_ref, logits.shape), 1.0, 0.0)
        valid = lax.broadcasted_iota(jnp.int32, logits.shape, 0) < 4
        grad_logits = jnp.where(valid, probs - onehot, 0.0).astype(BF16)
        grad_hidden = jnp.dot(grad_logits, second, preferred_element_type=F32)
        grad_pre = (grad_hidden * silu_slope(pre)).astype(BF16)
        hold[...] = jnp.zeros_like(hold)
        hold[0:8, :] = normed.astype(F32)
        hold[8:16, 0:channels] = grad_pre.astype(F32)
        hold[8:16, channels:] = hidden.astype(F32)
        hold[16:24, 0:languages] = grad_logits.astype(F32)
        lines_ref[...] = hold[...].astype(BF16)
        low = grad_pre[:, :half]
        high = grad_pre[:, half:]
        mine = jnp.where(core == 0, low, high)
        theirs = jnp.where(core == 0, high, low)
        grad_normed = lax.dot_general(mine, own_ref[...], dims, preferred_element_type=F32)
        grad_normed += lax.dot_general(theirs, other_ref[...], dims, preferred_element_type=F32)
        mean = jnp.mean(grad_normed * unit, axis=-1, keepdims=True)
        grad_pooled = r * (grad_normed - unit * mean)
        rev_ref[...] = -REVERSAL * grad_pooled / per_row(lens_ref, (8, 1)).astype(F32)


def critic_sums_kernel(band_rows, parts, sec_ref, yl_ref, core_ref, lines_ref, kept_ref, sent_ref, crit):
    n_yl, n_z, n_c = parts
    n_dp = n_yl * n_z * n_c
    features = lines_ref.shape[1]
    channels = features // 2
    padded = crit.shape[0] // n_dp
    share = channels // n_dp

    def grow(block):
        return jnp.concatenate([block, jnp.zeros_like(block)], axis=0).astype(BF16)

    def pick(shape, test):
        rows = lax.broadcasted_iota(jnp.int32, shape, 0)
        columns = lax.broadcasted_iota(jnp.int32, shape, 1)
        return jnp.where(test(rows, columns), 1.0, 0.0).astype(BF16)

    lines = lines_ref[...].astype(F32)
    base = sec_ref[0] * band_rows
    band = pick((features, 256), lambda i, j: (i == j + base) & (j < band_rows))
    nb = jnp.dot(grow(lines[0:8]), band, preferred_element_type=F32).astype(BF16)
    wide = (channels, n_dp * padded)
    columns = lax.broadcasted_iota(jnp.int32, (1, wide[1]), 1)
    slot = lax.div(columns, padded)
    inside = columns - slot * padded
    source = jnp.where(inside < share, slot * share + inside, -1)
    spread = jnp.where(lax.broadcasted_iota(jnp.int32, wide, 0) == source, 1.0, 0.0).astype(BF16)
    both = grow(lines[8:16])
    gp = jnp.dot(both[:, :channels], spread, preferred_element_type=F32).astype(BF16)
    hid = jnp.dot(both[:, channels:], spread, preferred_element_type=F32).astype(BF16)
    shift = pick((128, 256), lambda i, j: j == i + 192)
    gl = jnp.dot(grow(lines[16:24, :128]), shift, preferred_element_type=F32).astype(BF16)
    dims = (((0,), (0,)), ((), ()))
    crit[...] = lax.dot_general(gp, nb, dims, preferred_element_type=F32)
    crit[...] += lax.dot_general(hid, gl, dims, preferred_element_type=F32)

    def pack(z, _):
        for dy, dc, dest in places(parts, yl_ref, core_ref, z):
            piece = crit[pl.ds(pl.multiple_of(dest * padded, 16), padded), :].astype(BF16)
            (sent_ref if dc else kept_ref)[dy, z] = piece
        return 0

    lax.fori_loop(0, n_z, pack, 0)


def places(parts, yl_ref, core_ref, z):
    n_yl, n_z, n_c = parts
    found = []
    for dy in range(n_yl):
        for dc in range(n_c):
            yl = yl_ref[0] if dy == 0 else n_yl - 1 - yl_ref[0]
            c = core_ref[0] if dc == 0 else n_c - 1 - core_ref[0]
            found.append((dy, dc, (yl * n_z + z) * n_c + c))
    return found


def plus(left, right):
    return (left.astype(F32) + right.astype(F32)).astype(BF16)


def split_kernel(kept_ref, got_ref, own_ref, other_ref):
    own_ref[...] = plus(kept_ref[0], got_ref[0])
    if kept_ref.shape[0] > 1:
        other_ref[...] = plus(kept_ref[1], got_ref[1])


def add_kernel(left_ref, right_ref, out_ref):
    out_ref[...] = plus(left_ref[...], right_ref[...])


def pick_kernel(targets, sec_ref, moved_ref, held_ref, out_ref):
    gets = functools.reduce(jnp.logical_or, [sec_ref[0] == target for target in targets])

    @pl.when(gets)
    def _():
        out_ref[...] = moved_ref[...]

    @pl.when(jnp.logical_not(gets))
    def _():
        out_ref[...] = held_ref[...]


def finish_kernel(parts, yl_ref, core_ref, xn_ref, g_ref, h_ref, da_ref, *refs):
    outs, (down, up) = refs[:-2], refs[-2:]
    n_yl, n_z, n_c = parts
    features = xn_ref.shape[1]
    dims = (((0,), (0,)), ((), ()))
    width = 256
    for k in range(features // width):
        cols = pl.ds(k * width, width)
        down[cols, :] = lax.dot_general(xn_ref[:, cols], da_ref[...], dims, preferred_element_type=F32)
        up[cols, :] = lax.dot_general(g_ref[:, cols], h_ref[...], dims, preferred_element_type=F32)
    span = features // (n_yl * n_z * n_c)

    def pack(z, _):
        for dy, dc, dest in places(parts, yl_ref, core_ref, z):
            rows = pl.ds(pl.multiple_of(dest * span, 8), span)
            piece = jnp.concatenate([down[rows, :], up[rows, :]], axis=0)
            outs[dc * n_yl + dy][z] = piece.astype(BF16)
        return 0

    lax.fori_loop(0, n_z, pack, 0)


def join_kernel(sec_ref, *refs):
    *parts, out_ref = refs
    rows = parts[0].shape[0]

    @pl.when(sec_ref[0] % 2 == 1)
    def _():
        for i, ref in enumerate(parts):
            out_ref[i * rows : (i + 1) * rows, :] = ref[...]


def after(value, token):
    return lax.optimization_barrier((value, token))[0]


def swap(block, axis, size):
    return lax.ppermute(block, axis, [(i, size - 1 - i) for i in range(size)])


def body(parts, *args):
    return whole(parts, *args)


def whole(parts, section_in, top_grad, seq_lengths, lang_labels, norm_gain, w_down, w_up, critic_first, critic_second):
    n_yl, n_z, n_c = parts
    n_dp = n_yl * n_z * n_c
    sec = lax.axis_index(SEC)
    core = lax.axis_index("c")
    micros, seq_len, features = 4, 128, section_in.shape[-1]
    rank = w_down.shape[-1]
    rows = micros * seq_len
    chunks = rows // CHUNK
    x = section_in.reshape(rows, features)
    top = top_grad.reshape(rows, features)
    gain = norm_gain.reshape(1, features)
    wd = w_down[0]
    sec_s = sec.reshape(1).astype(jnp.int32)
    core_s = core.reshape(1).astype(jnp.int32)
    yl_s = lax.axis_index("yl").reshape(1).astype(jnp.int32)
    channels = critic_first.shape[1]
    half = channels // 2
    sds = jax.ShapeDtypeStruct

    lens = seq_lengths.reshape(micros)
    mine = call(
        half_kernel,
        sds((critic_first.shape[0], half), BF16),
        [SM, VM],
        (core_s, critic_first),
        0,
        1 << 19,
    )
    even = lax.ppermute(mine, SEC, [(i, i + 1) for i in range(0, SECTIONS, 2)])
    second = critic_second.T
    xn, h, a, q, pooled, wut, wdt, grads, inner = call(
        prepare_kernel,
        (
            sds((rows, features), BF16),
            sds((rows, rank), BF16),
            sds((rows, rank), F32),
            sds((rows, 128), F32),
            sds((8, features), F32),
            sds((features, rank), BF16),
            sds((rank, features), BF16),
            sds((rows, features), BF16),
            sds((rows, rank), BF16),
        ),
        [SM, SM] + [VM] * 4,
        (lens, yl_s, x, gain, wd, w_up[0]),
        2 * rows * features * rank,
        8 << 20,
    )

    three = SECTIONS // 2 - 1
    held = {}
    band_rows = critic_first.shape[0]
    share = channels // n_dp
    padded = -(-share // 16) * 16

    def join(token, *pieces):
        return call(
            join_kernel,
            sds((len(pieces) * pieces[0].shape[0], half), BF16),
            [SM] + [VM] * len(pieces),
            (after(sec_s, token), *pieces),
            0,
            2 << 20,
        )

    def side_work(step, token):
        if step == 0:
            held["pair"] = join(token, even, mine)
            held["far"] = [lax.ppermute(held["pair"], SEC, [(i, three)]) for i in (7, 5, 1)]
        elif step == 1:
            held["pooled"] = lax.ppermute(after(pooled, token), SEC, [(4, three)])
        elif step == 4:
            far = held["far"]
            held["own"] = join(token, far[2], held["pair"], far[1], far[0])
            pairs = [(three * 2, three * 2 + 1), (three * 2 + 1, three * 2)]
            held["other"] = lax.ppermute(held["own"], SEC + ("c",), pairs)
        elif step == 7:
            held["lines"], held["rev"] = call(
                critic_kernel,
                (sds((32, features), BF16), sds((8, features), F32)),
                [SM] * 4 + [VM] * 4,
                (
                    after(sec_s, token),
                    core_s,
                    lang_labels.reshape(micros),
                    lens,
                    held["pooled"],
                    held["own"],
                    held["other"],
                    second,
                ),
                1 << 27,
                4 << 20,
                scratch=[pltpu.VMEM((32, features), F32)],
            )
        if step in (10, 12, 14) and "moved" in held:
            targets, moved = held.pop("moved")
            held["lines"] = call(
                functools.partial(pick_kernel, targets),
                sds(held["lines"].shape, BF16),
                [SM, VM, VM],
                (after(sec_s, token), moved, held["lines"]),
                0,
                1 << 18,
            )
        if step in (8, 10, 12):
            lines = after(held["lines"], token)
            if step == 8:
                route = [(3, 7)]
            elif step == 10:
                route = [(3, 1), (7, 5)]
            else:
                route = [(i + 1, i) for i in range(0, SECTIONS, 2)]
            moved = lax.ppermute(lines, SEC, route)
            held["moved"] = ([target for _, target in route], moved)
        elif step == 14:
            kept, sent = call(
                functools.partial(critic_sums_kernel, band_rows, parts),
                (sds((n_yl, n_z, padded, rank), BF16),) * 2,
                [SM, SM, SM, VM],
                (after(sec_s, token), yl_s, core_s, held["lines"]),
                1 << 26,
                1 << 20,
                scratch=[pltpu.VMEM((n_dp * padded, rank), F32)],
            )
            held["kept"] = kept
            held["got"] = swap(sent, "c", n_c)
        elif step == 16:
            one = sds((n_z, padded, rank), BF16)
            own, other = call(split_kernel, (one, one), [VM, VM], (after(held["kept"], token), held["got"]), 0, 1 << 20)
            held["own_sum"] = own
            if n_yl == 2:
                held["other_sum"] = swap(other, "yl", n_yl)
        elif step == 18 and n_yl == 2:
            args = (after(held["own_sum"], token), held["other_sum"])
            held["own_sum"] = call(add_kernel, sds(args[0].shape, BF16), [VM, VM], args, 0, 1 << 20)

    steps = DELAY * (SECTIONS - 1) + chunks
    received = {}
    relay_route = [(i, i - 1) for i in range(1, SECTIONS)]
    for step in range(steps):
        has_top = step < chunks
        has_in = step >= DELAY
        first_rev = DELAY * (SECTIONS - 1 - three)
        has_rev = first_rev <= step < first_rev + chunks
        args = [sec_s, lens, x, a, q, gain, wut, wdt]
        specs = [SM, SM] + [VM] * 6
        if has_top:
            args.append(top)
        if has_in:
            args.append(received.pop(step - DELAY))
        if has_rev:
            args.append(held["rev"])
        args += [grads, inner]
        specs += [VM] * (len(args) - len(specs))
        passed = [len(args) - 2, len(args) - 1] + STAY
        outgoing, grads, inner, *stay = call(
            functools.partial(step_kernel, step, chunks, has_top, has_in, has_rev),
            (sds((CHUNK, features), BF16),) + tuple(sds(args[i].shape, args[i].dtype) for i in passed),
            specs,
            tuple(args),
            4 * CHUNK * features * rank,
            3 << 20,
            aliases={i: k + 1 for k, i in enumerate(passed)},
        )
        x, a, q, wut, wdt = stay
        if step < steps - DELAY:
            received[step] = lax.ppermute(outgoing, SEC, relay_route)
        side_work(step, outgoing)

    span = features // n_dp
    piece = sds((n_z, 2 * span, rank), BF16)
    packed = call(
        functools.partial(finish_kernel, parts),
        (piece,) * (n_yl * n_c),
        [SM, SM] + [VM] * 4,
        (yl_s, core_s, xn, grads, h, inner),
        4 * rows * features * rank,
        8 << 20,
        scratch=[pltpu.VMEM((features, rank), F32)] * 2,
    )

    kept, sent = packed[:n_yl], packed[n_yl:]
    halves = [None] * n_yl
    for i in reversed(range(n_yl)):
        arrived = swap(sent[i], "c", n_c)
        args = (kept[i], arrived)
        halves[i] = call(add_kernel, sds(arrived.shape, BF16), [VM, VM], args, 0, 2 << 20)
    summed = halves[0]
    crit = after(held["own_sum"], packed[-1])
    if n_z > 1:
        crit = lax.all_to_all(crit, "z", 0, 0, tiled=True)
    if n_yl == 2:
        summed = plus(summed, swap(halves[1], "yl", n_yl))
    if n_z > 1:
        summed = lax.all_to_all(summed, "z", 0, 0, tiled=True)
    total = jnp.sum(summed.astype(F32), axis=0)
    down = total[:span]
    up = total[span:].T
    crit = jnp.sum(crit.astype(F32), axis=0)[:share]
    dp_place = lax.axis_index(("yl", "z", "c"))
    wd_own = lax.dynamic_slice_in_dim(wd, dp_place * span, span, 0).astype(F32)
    gain_own = lax.dynamic_slice_in_dim(gain[0], dp_place * span, span, 0)
    grad_gain = jnp.sum(down * wd_own, axis=1) / gain_own
    first = crit[:, :band_rows].T
    second_grad = crit[:, 192 : 192 + critic_second.shape[1]]
    return (down[None], up[None], grad_gain[None], first, second_grad)


def solution(mesh):
    n_dp = mesh.shape["dp"]
    parts = (2, n_dp // 4, 2) if n_dp >= 8 else (1, n_dp // 2, 2)
    fine = Mesh(mesh.devices.reshape((SECTIONS // 2, 2) + parts), SEC + ("yl", "z", "c"))
    dp = ("yl", "z", "c")
    return jax.shard_map(
        functools.partial(body, parts),
        mesh=fine,
        in_specs=(
            P(SEC, None, dp, None, None),
            P(None, dp, None, None),
            P(None, dp),
            P(None, dp),
            P(SEC, None),
            P(SEC, None, None),
            P(SEC, None, None),
            P(SEC, None),
            P(),
        ),
        out_specs=(P(SEC, dp, None), P(SEC, None, dp), P(SEC, dp), P(SEC, dp), P(dp, None)),
        check_vma=False,
    )
```

```python
import functools
import math

import jax
import jax.numpy as jnp
from jax import lax
from jax.experimental import pallas as pl
from jax.experimental.pallas import tpu as pltpu
from jax.sharding import Mesh, PartitionSpec as P


EPSILON = 1e-06
REVERSAL = 0.5
SECTIONS = 8
CHUNK = 64
STAY = [2, 3, 4, 6, 7]
DELAY = 2
SEC = ("x", "yh")
F32 = jnp.float32
BF16 = jnp.bfloat16
VM = pl.BlockSpec(memory_space=pltpu.VMEM)
SM = pl.BlockSpec(memory_space=pltpu.SMEM)


def silu_slope(pre_act):
    sigma = jax.nn.sigmoid(pre_act)
    return sigma * (1.0 + pre_act * (1.0 - sigma))


def call(kernel, out_shape, in_specs, args, flops, moved, aliases=None, scratch=(), limit=16):
    return pl.pallas_call(
        kernel,
        out_shape=out_shape,
        in_specs=in_specs,
        out_specs=jax.tree.map(lambda _: VM, out_shape),
        input_output_aliases=aliases or {},
        scratch_shapes=scratch,
        compiler_params=pltpu.CompilerParams(vmem_limit_bytes=limit << 20),
        cost_estimate=pl.CostEstimate(flops=flops, bytes_accessed=moved, transcendentals=0),
    )(*args)


def half_kernel(core_ref, first_ref, mine_ref):
    half = mine_ref.shape[1]
    for c in range(2):

        @pl.when(core_ref[0] == c)
        def _():
            mine_ref[...] = first_ref[:, c * half : (c + 1) * half]


def prepare_kernel(lens_ref, _sec, _yl, _zl, x_ref, gain_ref, wd_ref, wu_ref, *refs):
    xn_ref, h_ref, a_ref, q_ref, pooled_ref, wut_ref, wdt_ref, _, _ = refs
    micros, seq_len = 4, 128
    gain = gain_ref[0:1, :]
    wut_ref[...] = wu_ref[...].T
    wdt_ref[...] = wd_ref[...].T
    pooled_ref[...] = jnp.zeros_like(pooled_ref)
    positions = lax.broadcasted_iota(jnp.int32, (seq_len, 1), 0)
    for m in range(micros):
        rows = pl.ds(m * seq_len, seq_len)
        values = x_ref[rows, :].astype(F32)
        count = lens_ref[m]
        total = jnp.sum(jnp.where(positions < count, values, 0.0), axis=0, keepdims=True)
        pooled_ref[m : m + 1, :] = total / count.astype(F32)
        q = lax.rsqrt(jnp.mean(values * values, axis=-1, keepdims=True) + EPSILON)
        normed = (values * q * gain).astype(BF16)
        xn_ref[rows, :] = normed
        a = jnp.dot(normed, wd_ref[...], preferred_element_type=F32)
        a_ref[rows, :] = a
        h_ref[rows, :] = (a * jax.nn.sigmoid(a)).astype(BF16)
        q_ref[rows, :] = jnp.broadcast_to(q, (seq_len, 128))


def step_kernel(step, chunks, has_top, has_in, has_rev, *refs):
    refs = list(refs)
    sec_ref, lens_ref, x_ref, a_ref, q_ref, gain_ref, wut_ref, wdt_ref = refs[:8]
    refs = refs[8:]
    top_ref = refs.pop(0) if has_top else None
    in_ref = refs.pop(0) if has_in else None
    rev_ref = refs.pop(0) if has_rev else None
    out_ref, g_ref, da_ref = refs[2:5]
    features = x_ref.shape[1]
    sec = sec_ref[0]
    place = step - DELAY * (SECTIONS - 1 - sec)
    live = (place >= 0) & (place < chunks)
    place = jnp.clip(place, 0, chunks - 1)
    rows = pl.ds(pl.multiple_of(place * CHUNK, CHUNK), CHUNK)

    if has_top:

        @pl.when(live & (sec == SECTIONS - 1))
        def _():
            g_ref[rows, :] = top_ref[rows, :]

    if has_in:

        @pl.when(live & (sec < SECTIONS - 1))
        def _():
            g_ref[rows, :] = in_ref[...]

    if has_rev:

        @pl.when(live & (sec == SECTIONS // 2 - 1))
        def _():
            per = 128 // CHUNK
            micro = lax.div(place, per)
            first = lax.rem(place, per) * CHUNK
            positions = lax.broadcasted_iota(jnp.int32, (CHUNK, 1), 0) + first
            extra = jnp.where(positions < lens_ref[micro], rev_ref[pl.ds(micro, 1), :], 0.0)
            g_ref[rows, :] = (in_ref[...].astype(F32) + extra).astype(BF16)

    @pl.when(live)
    def _():
        g = g_ref[rows, :]
        a = a_ref[rows, :]
        q = q_ref[rows, 0:1]
        dh = jnp.dot(g, wut_ref[...], preferred_element_type=F32)
        da = (dh * silu_slope(a)).astype(BF16)
        da_ref[rows, :] = da
        mean = jnp.sum(da.astype(F32) * a, axis=-1, keepdims=True) * (1.0 / features)
        dxn = jnp.dot(da, wdt_ref[...], preferred_element_type=F32)
        x = x_ref[rows, :].astype(F32)
        out = g.astype(F32) + q * (dxn * gain_ref[0:1, :]) - x * (q * q * mean)
        out_ref[...] = out.astype(BF16)


def per_row(ref, shape):
    rows = lax.broadcasted_iota(jnp.int32, shape, 0)
    column = jnp.ones(shape, jnp.int32)
    for m in range(4):
        column = jnp.where(rows == m, ref[m], column)
    return column


def critic_kernel(
    sec_ref, core_ref, labels_ref, lens_ref, pooled_ref, own_ref, other_ref, second_ref, lines_ref, rev_ref, hold
):
    half = own_ref.shape[1]
    channels = 2 * half
    languages = second_ref.shape[0]

    @pl.when(sec_ref[0] == SECTIONS // 2 - 1)
    def _():
        pooled = pooled_ref[...].astype(BF16).astype(F32)
        r = lax.rsqrt(jnp.mean(pooled * pooled, axis=-1, keepdims=True) + EPSILON)
        unit = pooled * r
        normed = unit.astype(BF16)
        core = core_ref[0]
        pre_own = jnp.dot(normed, own_ref[...], preferred_element_type=F32)
        pre_other = jnp.dot(normed, other_ref[...], preferred_element_type=F32)
        low = jnp.where(core == 0, pre_own, pre_other)
        high = jnp.where(core == 0, pre_other, pre_own)
        pre = jnp.concatenate([low, high], axis=1)
        hidden = (pre * jax.nn.sigmoid(pre)).astype(BF16)
        second = second_ref[...]
        dims = (((1,), (1,)), ((), ()))
        logits = lax.dot_general(hidden, second, dims, preferred_element_type=F32)
        exponent = jnp.exp(logits)
        probs = exponent / jnp.sum(exponent, axis=-1, keepdims=True)
        lanes = lax.broadcasted_iota(jnp.int32, logits.shape, 1)
        onehot = jnp.where(lanes == per_row(labels_ref, logits.shape), 1.0, 0.0)
        valid = lax.broadcasted_iota(jnp.int32, logits.shape, 0) < 4
        grad_logits = jnp.where(valid, probs - onehot, 0.0).astype(BF16)
        grad_hidden = jnp.dot(grad_logits, second, preferred_element_type=F32)
        grad_pre = (grad_hidden * silu_slope(pre)).astype(BF16)
        hold[...] = jnp.zeros_like(hold)
        hold[0:8, :] = normed.astype(F32)
        hold[8:16, 0:channels] = grad_pre.astype(F32)
        hold[8:16, channels:] = hidden.astype(F32)
        hold[16:24, 0:languages] = grad_logits.astype(F32)
        lines_ref[...] = hold[...].astype(BF16)
        low = grad_pre[:, :half]
        high = grad_pre[:, half:]
        mine = jnp.where(core == 0, low, high)
        theirs = jnp.where(core == 0, high, low)
        grad_normed = lax.dot_general(mine, own_ref[...], dims, preferred_element_type=F32)
        grad_normed += lax.dot_general(theirs, other_ref[...], dims, preferred_element_type=F32)
        mean = jnp.mean(grad_normed * unit, axis=-1, keepdims=True)
        grad_pooled = r * (grad_normed - unit * mean)
        rev_ref[...] = -REVERSAL * grad_pooled / per_row(lens_ref, (8, 1)).astype(F32)


def critic_sums_kernel(band_rows, parts, sec_ref, yl_ref, z_ref, core_ref, lines_ref, kept_ref, sent_ref, crit):
    n_dp = math.prod(parts)
    n_z = parts[1]
    features = lines_ref.shape[1]
    channels = features // 2
    padded = crit.shape[0] // n_dp
    share = channels // n_dp

    def grow(block):
        return jnp.concatenate([block, jnp.zeros_like(block)], axis=0).astype(BF16)

    def pick(shape, test):
        rows = lax.broadcasted_iota(jnp.int32, shape, 0)
        columns = lax.broadcasted_iota(jnp.int32, shape, 1)
        return jnp.where(test(rows, columns), 1.0, 0.0).astype(BF16)

    lines = lines_ref[...].astype(F32)
    base = sec_ref[0] * band_rows
    band = pick((features, 256), lambda i, j: (i == j + base) & (j < band_rows))
    nb = jnp.dot(grow(lines[0:8]), band, preferred_element_type=F32).astype(BF16)
    wide = (channels, n_dp * padded)
    columns = lax.broadcasted_iota(jnp.int32, (1, wide[1]), 1)
    slot = lax.div(columns, padded)
    inside = columns - slot * padded
    source = jnp.where(inside < share, slot * share + inside, -1)
    spread = jnp.where(lax.broadcasted_iota(jnp.int32, wide, 0) == source, 1.0, 0.0).astype(BF16)
    both = grow(lines[8:16])
    gp = jnp.dot(both[:, :channels], spread, preferred_element_type=F32).astype(BF16)
    hid = jnp.dot(both[:, channels:], spread, preferred_element_type=F32).astype(BF16)
    shift = pick((128, 256), lambda i, j: j == i + 192)
    gl = jnp.dot(grow(lines[16:24, :128]), shift, preferred_element_type=F32).astype(BF16)
    dims = (((0,), (0,)), ((), ()))
    crit[...] = lax.dot_general(gp, nb, dims, preferred_element_type=F32)
    crit[...] += lax.dot_general(hid, gl, dims, preferred_element_type=F32)

    for i in range(n_z):
        for dy, dc, dest in places(parts, yl_ref, core_ref, jnp.bitwise_xor(z_ref[0], mirrored(i, n_z))):
            piece = crit[pl.ds(pl.multiple_of(dest * padded, 16), padded), :].astype(BF16)
            (sent_ref if dc else kept_ref)[dy, i] = piece


def places(parts, yl_ref, core_ref, z):
    n_yl, n_z, n_c = parts
    found = []
    for dy in range(n_yl):
        for dc in range(n_c):
            yl = yl_ref[0] if dy == 0 else n_yl - 1 - yl_ref[0]
            c = core_ref[0] if dc == 0 else n_c - 1 - core_ref[0]
            found.append((dy, dc, (yl * n_z + z) * n_c + c))
    return found


def mirrored(i, n):
    return sum(((i >> b) & 1) * (n >> (b + 1)) for b in range(n.bit_length() - 1))


def plus(left, right):
    return (left.astype(F32) + right.astype(F32)).astype(BF16)


def split_kernel(kept_ref, got_ref, own_ref, other_ref):
    own_ref[...] = plus(kept_ref[0], got_ref[0])
    if kept_ref.shape[0] > 1:
        other_ref[...] = plus(kept_ref[1], got_ref[1])


def fold_kernel(left_ref, right_ref, low_ref, high_ref):
    total = plus(left_ref[...], right_ref[...])
    half = low_ref.shape[0]
    low_ref[...] = total[:half]
    high_ref[...] = total[half:]


def add_kernel(left_ref, right_ref, out_ref):
    out_ref[...] = plus(left_ref[...], right_ref[...])


def pick_kernel(targets, sec_ref, moved_ref, held_ref, out_ref):
    gets = functools.reduce(jnp.logical_or, [sec_ref[0] == target for target in targets])

    @pl.when(gets)
    def _():
        out_ref[...] = moved_ref[...]

    @pl.when(jnp.logical_not(gets))
    def _():
        out_ref[...] = held_ref[...]


def finish_kernel(parts, yl_ref, core_ref, xn_ref, g_ref, h_ref, da_ref, *refs):
    outs, (down, up) = refs[:-2], refs[-2:]
    n_yl, n_z, _ = parts
    features = xn_ref.shape[1]
    dims = (((0,), (0,)), ((), ()))
    width = 256
    for k in range(features // width):
        cols = pl.ds(k * width, width)
        down[cols, :] = lax.dot_general(xn_ref[:, cols], da_ref[...], dims, preferred_element_type=F32)
        up[cols, :] = lax.dot_general(g_ref[:, cols], h_ref[...], dims, preferred_element_type=F32)
    span = features // math.prod(parts)

    def pack(z, _):
        for dy, dc, dest in places(parts, yl_ref, core_ref, z):
            rows = pl.ds(pl.multiple_of(dest * span, 8), span)
            piece = jnp.concatenate([down[rows, :], up[rows, :]], axis=0)
            outs[dc * n_yl + dy][z] = piece.astype(BF16)
        return 0

    lax.fori_loop(0, n_z, pack, 0)


def join_kernel(sec_ref, *refs):
    *parts, out_ref = refs
    rows = parts[0].shape[0]

    @pl.when(sec_ref[0] % 2 == 1)
    def _():
        for i, ref in enumerate(parts):
            out_ref[i * rows : (i + 1) * rows, :] = ref[...]


def after(value, token):
    return lax.optimization_barrier((value, token))[0]


def swap(block, axis, size):
    return lax.ppermute(block, axis, [(i, size - 1 - i) for i in range(size)])


def body(parts, *args):
    return whole(parts, *args)


def whole(parts, section_in, top_grad, seq_lengths, lang_labels, norm_gain, w_down, w_up, critic_first, critic_second):
    n_yl, n_z, n_c = parts
    n_dp = n_yl * n_z * n_c
    sec = lax.axis_index(SEC)
    core = lax.axis_index("c")
    micros, seq_len, features = 4, 128, section_in.shape[-1]
    rank = w_down.shape[-1]
    rows = micros * seq_len
    chunks = rows // CHUNK
    x = section_in.reshape(rows, features)
    top = top_grad.reshape(rows, features)
    gain = norm_gain.reshape(1, features)
    wd = w_down[0]
    sec_s = sec.reshape(1).astype(jnp.int32)
    core_s = core.reshape(1).astype(jnp.int32)
    yl_s = lax.axis_index("yl").reshape(1).astype(jnp.int32)
    z_s = lax.axis_index("z").reshape(1).astype(jnp.int32)
    channels = critic_first.shape[1]
    half = channels // 2
    sds = jax.ShapeDtypeStruct

    lens = seq_lengths.reshape(micros)
    mine = call(
        half_kernel,
        sds((critic_first.shape[0], half), BF16),
        [SM, VM],
        (core_s, critic_first),
        0,
        1 << 19,
    )
    even = lax.ppermute(mine, SEC, [(i, i + 1) for i in range(0, SECTIONS, 2)])
    second = critic_second.T
    xn, h, a, q, pooled, wut, wdt, grads, inner = call(
        prepare_kernel,
        (
            sds((rows, features), BF16),
            sds((rows, rank), BF16),
            sds((rows, rank), F32),
            sds((rows, 128), F32),
            sds((8, features), F32),
            sds((features, rank), BF16),
            sds((rank, features), BF16),
            sds((rows, features), BF16),
            sds((rows, rank), BF16),
        ),
        [SM] * 4 + [VM] * 4,
        (lens, sec_s, yl_s, z_s, x, gain, wd, w_up[0]),
        2 * rows * features * rank,
        8 << 20,
    )

    three = SECTIONS // 2 - 1
    held = {}
    band_rows = critic_first.shape[0]
    share = channels // n_dp
    padded = -(-share // 16) * 16

    def join(token, *pieces):
        return call(
            join_kernel,
            sds((len(pieces) * pieces[0].shape[0], half), BF16),
            [SM] + [VM] * len(pieces),
            (after(sec_s, token), *pieces),
            0,
            2 << 20,
        )

    def side_work(step, token):
        if step == 0:
            held["pair"] = join(token, even, mine)
            held["far"] = [lax.ppermute(held["pair"], SEC, [(i, three)]) for i in (7, 5, 1)]
        elif step == 1:
            held["pooled"] = lax.ppermute(after(pooled, token), SEC, [(4, three)])
        elif step == 5:
            far = held["far"]
            held["own"] = join(token, far[2], held["pair"], far[1], far[0])
            pairs = [(three * 2, three * 2 + 1), (three * 2 + 1, three * 2)]
            held["other"] = lax.ppermute(held["own"], SEC + ("c",), pairs)
        elif step == 7:
            held["lines"], held["rev"] = call(
                critic_kernel,
                (sds((32, features), BF16), sds((8, features), F32)),
                [SM] * 4 + [VM] * 4,
                (
                    after(sec_s, token),
                    core_s,
                    lang_labels.reshape(micros),
                    lens,
                    held["pooled"],
                    held["own"],
                    held["other"],
                    second,
                ),
                1 << 27,
                4 << 20,
                scratch=[pltpu.VMEM((32, features), F32)],
            )
        if step in (10, 12, 14) and "moved" in held:
            targets, moved = held.pop("moved")
            held["lines"] = call(
                functools.partial(pick_kernel, targets),
                sds(held["lines"].shape, BF16),
                [SM, VM, VM],
                (after(sec_s, token), moved, held["lines"]),
                0,
                1 << 18,
            )
        if step in (8, 10, 12):
            lines = after(held["lines"], token)
            if step == 8:
                route = [(3, 7)]
            elif step == 10:
                route = [(3, 1), (7, 5)]
            else:
                route = [(i + 1, i) for i in range(0, SECTIONS, 2)]
            moved = lax.ppermute(lines, SEC, route)
            held["moved"] = ([target for _, target in route], moved)
        elif step == 14:
            kept, sent = call(
                functools.partial(critic_sums_kernel, band_rows, parts),
                (sds((n_yl, n_z, padded, rank), BF16),) * 2,
                [SM, SM, SM, SM, VM],
                (after(sec_s, token), yl_s, z_s, core_s, held["lines"]),
                1 << 26,
                1 << 20,
                scratch=[pltpu.VMEM((n_dp * padded, rank), F32)],
            )
            held["kept"] = kept
            held["got"] = swap(sent, "c", n_c)
        elif step == 16:
            one = sds((n_z, padded, rank), BF16)
            own, other = call(split_kernel, (one, one), [VM, VM], (after(held["kept"], token), held["got"]), 0, 1 << 20)
            held["own_sum"] = own
            if n_yl == 2:
                held["other_sum"] = swap(other, "yl", n_yl)
        elif step == 18 and n_yl == 2:
            fold(after(held["own_sum"], token), held["other_sum"], 1)

    def fold(left, right, bit):
        size = left.shape[0]
        if size == 1:
            held["own_sum"] = call(add_kernel, sds(left.shape, BF16), [VM, VM], (left, right), 0, 1 << 18)
            return
        one = sds((size // 2,) + left.shape[1:], BF16)
        held["own_sum"], high = call(fold_kernel, (one, one), [VM, VM], (left, right), 0, 1 << 20)
        held["other_sum"] = lax.ppermute(high, "z", [(i, i ^ bit) for i in range(n_z)])

    steps = DELAY * (SECTIONS - 1) + chunks
    received = {}
    relay_route = [(i, i - 1) for i in range(1, SECTIONS)]
    for step in range(steps):
        has_top = step < chunks
        has_in = step >= DELAY
        first_rev = DELAY * (SECTIONS - 1 - three)
        has_rev = first_rev <= step < first_rev + chunks
        args = [sec_s, lens, x, a, q, gain, wut, wdt]
        specs = [SM, SM] + [VM] * 6
        if has_top:
            args.append(top)
        if has_in:
            args.append(received.pop(step - DELAY))
        if has_rev:
            args.append(held["rev"])
        args += [grads, inner]
        specs += [VM] * (len(args) - len(specs))
        passed = [len(args) - 2, len(args) - 1] + STAY
        outgoing, grads, inner, *stay = call(
            functools.partial(step_kernel, step, chunks, has_top, has_in, has_rev),
            (sds((CHUNK, features), BF16),) + tuple(sds(args[i].shape, args[i].dtype) for i in passed),
            specs,
            tuple(args),
            4 * CHUNK * features * rank,
            3 << 20,
            aliases={i: k + 1 for k, i in enumerate(passed)},
        )
        x, a, q, wut, wdt = stay
        if step < steps - DELAY:
            received[step] = lax.ppermute(outgoing, SEC, relay_route)
        side_work(step, outgoing)

    span = features // n_dp
    piece = sds((n_z, 2 * span, rank), BF16)
    packed = call(
        functools.partial(finish_kernel, parts),
        (piece,) * (n_yl * n_c),
        [SM] * 2 + [VM] * 4,
        (yl_s, core_s, xn, grads, h, inner),
        4 * rows * features * rank,
        8 << 20,
        scratch=[pltpu.VMEM((features, rank), F32)] * 2,
    )

    kept, sent = packed[:n_yl], packed[n_yl:]
    halves = [None] * n_yl
    for i in reversed(range(n_yl)):
        arrived = swap(sent[i], "c", n_c)
        args = (kept[i], arrived)
        halves[i] = call(add_kernel, sds(arrived.shape, BF16), [VM, VM], args, 0, 2 << 20)
    summed = halves[0]
    if n_yl == 2:
        arrived = swap(halves[1], "yl", n_yl)
        bit = 2
        while bit <= n_z:
            fold(held["own_sum"], held["other_sum"], bit)
            bit *= 2
        summed = call(add_kernel, sds(arrived.shape, BF16), [VM, VM], (summed, arrived), 0, 2 << 20)
    if n_z > 1:
        summed = lax.all_to_all(summed, "z", 0, 0, tiled=True)
    total = jnp.sum(summed.astype(F32), axis=0)
    down = total[:span]
    up = total[span:].T
    crit = held["own_sum"][0, :share].astype(F32)
    dp_place = lax.axis_index(("yl", "z", "c"))
    wd_own = lax.dynamic_slice_in_dim(wd, dp_place * span, span, 0).astype(F32)
    gain_own = lax.dynamic_slice_in_dim(gain[0], dp_place * span, span, 0)
    grad_gain = jnp.sum(down * wd_own, axis=1) / gain_own
    first = crit[:, :band_rows].T
    second_grad = crit[:, 192 : 192 + critic_second.shape[1]]
    return (down[None], up[None], grad_gain[None], first, second_grad)


def solution(mesh):
    n_dp = mesh.shape["dp"]
    parts = (2, n_dp // 4, 2) if n_dp >= 4 else (1, n_dp // 2, 2)
    fine = Mesh(mesh.devices.reshape((SECTIONS // 2, 2) + parts), SEC + ("yl", "z", "c"))
    dp = ("yl", "z", "c")
    return jax.shard_map(
        functools.partial(body, parts),
        mesh=fine,
        in_specs=(
            P(SEC, None, dp, None, None),
            P(None, dp, None, None),
            P(None, dp),
            P(None, dp),
            P(SEC, None),
            P(SEC, None, None),
            P(SEC, None, None),
            P(SEC, None),
            P(),
        ),
        out_specs=(P(SEC, dp, None), P(SEC, None, dp), P(SEC, dp), P(SEC, dp), P(dp, None)),
        check_vma=False,
    )
```

```python
import functools
import math

import jax
import jax.numpy as jnp
from jax import lax
from jax.experimental import pallas as pl
from jax.experimental.pallas import tpu as pltpu
from jax.sharding import Mesh, PartitionSpec as P


EPSILON = 1e-06
REVERSAL = 0.5
SECTIONS = 8
CHUNK = 64
STAY = [2, 3, 4, 6, 7]
DELAY = 2
SEC = ("x", "yh")
F32 = jnp.float32
BF16 = jnp.bfloat16
VM = pl.BlockSpec(memory_space=pltpu.VMEM)
SM = pl.BlockSpec(memory_space=pltpu.SMEM)


def silu_slope(pre_act):
    sigma = jax.nn.sigmoid(pre_act)
    return sigma * (1.0 + pre_act * (1.0 - sigma))


def call(kernel, out_shape, in_specs, args, flops, moved, aliases=None, scratch=(), limit=16):
    return pl.pallas_call(
        kernel,
        out_shape=out_shape,
        in_specs=in_specs,
        out_specs=jax.tree.map(lambda _: VM, out_shape),
        input_output_aliases=aliases or {},
        scratch_shapes=scratch,
        compiler_params=pltpu.CompilerParams(vmem_limit_bytes=limit << 20),
        cost_estimate=pl.CostEstimate(flops=flops, bytes_accessed=moved, transcendentals=0),
    )(*args)


def half_kernel(core_ref, first_ref, mine_ref):
    half = mine_ref.shape[1]
    for c in range(2):

        @pl.when(core_ref[0] == c)
        def _():
            mine_ref[...] = first_ref[:, c * half : (c + 1) * half]


def prepare_kernel(lens_ref, _sec, _yl, _zl, x_ref, gain_ref, wd_ref, wu_ref, *refs):
    xn_ref, h_ref, a_ref, q_ref, pooled_ref, wut_ref, wdt_ref, _, _ = refs
    micros, seq_len = 4, 128
    gain = gain_ref[0:1, :]
    wut_ref[...] = wu_ref[...].T
    wdt_ref[...] = wd_ref[...].T
    pooled_ref[...] = jnp.zeros_like(pooled_ref)
    positions = lax.broadcasted_iota(jnp.int32, (seq_len, 1), 0)
    for m in range(micros):
        rows = pl.ds(m * seq_len, seq_len)
        values = x_ref[rows, :].astype(F32)
        count = lens_ref[m]
        total = jnp.sum(jnp.where(positions < count, values, 0.0), axis=0, keepdims=True)
        pooled_ref[m : m + 1, :] = total / count.astype(F32)
        q = lax.rsqrt(jnp.mean(values * values, axis=-1, keepdims=True) + EPSILON)
        normed = (values * q * gain).astype(BF16)
        xn_ref[rows, :] = normed
        a = jnp.dot(normed, wd_ref[...], preferred_element_type=F32)
        a_ref[rows, :] = a
        h_ref[rows, :] = (a * jax.nn.sigmoid(a)).astype(BF16)
        q_ref[rows, :] = jnp.broadcast_to(q, (seq_len, 128))


def step_kernel(step, chunks, has_top, has_in, has_rev, *refs):
    refs = list(refs)
    sec_ref, lens_ref, x_ref, a_ref, q_ref, gain_ref, wut_ref, wdt_ref = refs[:8]
    refs = refs[8:]
    top_ref = refs.pop(0) if has_top else None
    in_ref = refs.pop(0) if has_in else None
    rev_ref = refs.pop(0) if has_rev else None
    out_ref, g_ref, da_ref = refs[2:5]
    features = x_ref.shape[1]
    sec = sec_ref[0]
    place = step - DELAY * (SECTIONS - 1 - sec)
    live = (place >= 0) & (place < chunks)
    place = jnp.clip(place, 0, chunks - 1)
    rows = pl.ds(pl.multiple_of(place * CHUNK, CHUNK), CHUNK)

    if has_top:

        @pl.when(live & (sec == SECTIONS - 1))
        def _():
            g_ref[rows, :] = top_ref[rows, :]

    if has_in:

        @pl.when(live & (sec < SECTIONS - 1))
        def _():
            g_ref[rows, :] = in_ref[...]

    if has_rev:

        @pl.when(live & (sec == SECTIONS // 2 - 1))
        def _():
            per = 128 // CHUNK
            micro = lax.div(place, per)
            first = lax.rem(place, per) * CHUNK
            positions = lax.broadcasted_iota(jnp.int32, (CHUNK, 1), 0) + first
            extra = jnp.where(positions < lens_ref[micro], rev_ref[pl.ds(micro, 1), :], 0.0)
            g_ref[rows, :] = (in_ref[...].astype(F32) + extra).astype(BF16)

    @pl.when(live)
    def _():
        g = g_ref[rows, :]
        a = a_ref[rows, :]
        q = q_ref[rows, 0:1]
        dh = jnp.dot(g, wut_ref[...], preferred_element_type=F32)
        da = (dh * silu_slope(a)).astype(BF16)
        da_ref[rows, :] = da
        mean = jnp.sum(da.astype(F32) * a, axis=-1, keepdims=True) * (1.0 / features)
        dxn = jnp.dot(da, wdt_ref[...], preferred_element_type=F32)
        x = x_ref[rows, :].astype(F32)
        out = g.astype(F32) + q * (dxn * gain_ref[0:1, :]) - x * (q * q * mean)
        out_ref[...] = out.astype(BF16)


def per_row(ref, shape):
    rows = lax.broadcasted_iota(jnp.int32, shape, 0)
    column = jnp.ones(shape, jnp.int32)
    for m in range(4):
        column = jnp.where(rows == m, ref[m], column)
    return column


def critic_kernel(
    sec_ref, core_ref, labels_ref, lens_ref, pooled_ref, own_ref, other_ref, second_ref, lines_ref, rev_ref, hold
):
    half = own_ref.shape[1]
    channels = 2 * half
    languages = second_ref.shape[0]

    @pl.when(sec_ref[0] == SECTIONS // 2 - 1)
    def _():
        pooled = pooled_ref[...].astype(BF16).astype(F32)
        r = lax.rsqrt(jnp.mean(pooled * pooled, axis=-1, keepdims=True) + EPSILON)
        unit = pooled * r
        normed = unit.astype(BF16)
        core = core_ref[0]
        pre_own = jnp.dot(normed, own_ref[...], preferred_element_type=F32)
        pre_other = jnp.dot(normed, other_ref[...], preferred_element_type=F32)
        low = jnp.where(core == 0, pre_own, pre_other)
        high = jnp.where(core == 0, pre_other, pre_own)
        pre = jnp.concatenate([low, high], axis=1)
        hidden = (pre * jax.nn.sigmoid(pre)).astype(BF16)
        second = second_ref[...]
        dims = (((1,), (1,)), ((), ()))
        logits = lax.dot_general(hidden, second, dims, preferred_element_type=F32)
        exponent = jnp.exp(logits)
        probs = exponent / jnp.sum(exponent, axis=-1, keepdims=True)
        lanes = lax.broadcasted_iota(jnp.int32, logits.shape, 1)
        onehot = jnp.where(lanes == per_row(labels_ref, logits.shape), 1.0, 0.0)
        valid = lax.broadcasted_iota(jnp.int32, logits.shape, 0) < 4
        grad_logits = jnp.where(valid, probs - onehot, 0.0).astype(BF16)
        grad_hidden = jnp.dot(grad_logits, second, preferred_element_type=F32)
        grad_pre = (grad_hidden * silu_slope(pre)).astype(BF16)
        hold[...] = jnp.zeros_like(hold)
        hold[0:8, :] = normed.astype(F32)
        hold[8:16, 0:channels] = grad_pre.astype(F32)
        hold[8:16, channels:] = hidden.astype(F32)
        hold[16:24, 0:languages] = grad_logits.astype(F32)
        lines_ref[...] = hold[...].astype(BF16)
        low = grad_pre[:, :half]
        high = grad_pre[:, half:]
        mine = jnp.where(core == 0, low, high)
        theirs = jnp.where(core == 0, high, low)
        grad_normed = lax.dot_general(mine, own_ref[...], dims, preferred_element_type=F32)
        grad_normed += lax.dot_general(theirs, other_ref[...], dims, preferred_element_type=F32)
        mean = jnp.mean(grad_normed * unit, axis=-1, keepdims=True)
        grad_pooled = r * (grad_normed - unit * mean)
        rev_ref[...] = -REVERSAL * grad_pooled / per_row(lens_ref, (8, 1)).astype(F32)


def critic_sums_kernel(band_rows, parts, sec_ref, yl_ref, zl_ref, core_ref, lines_ref, kept_ref, sent_ref, crit):
    n_dp = math.prod(parts)
    n_z = parts[1] * parts[2]
    features = lines_ref.shape[1]
    channels = features // 2
    padded = crit.shape[0] // n_dp
    share = channels // n_dp

    def grow(block):
        return jnp.concatenate([block, jnp.zeros_like(block)], axis=0).astype(BF16)

    def pick(shape, test):
        rows = lax.broadcasted_iota(jnp.int32, shape, 0)
        columns = lax.broadcasted_iota(jnp.int32, shape, 1)
        return jnp.where(test(rows, columns), 1.0, 0.0).astype(BF16)

    lines = lines_ref[...].astype(F32)
    base = sec_ref[0] * band_rows
    band = pick((features, 256), lambda i, j: (i == j + base) & (j < band_rows))
    nb = jnp.dot(grow(lines[0:8]), band, preferred_element_type=F32).astype(BF16)
    wide = (channels, n_dp * padded)
    columns = lax.broadcasted_iota(jnp.int32, (1, wide[1]), 1)
    slot = lax.div(columns, padded)
    inside = columns - slot * padded
    source = jnp.where(inside < share, slot * share + inside, -1)
    spread = jnp.where(lax.broadcasted_iota(jnp.int32, wide, 0) == source, 1.0, 0.0).astype(BF16)
    both = grow(lines[8:16])
    gp = jnp.dot(both[:, :channels], spread, preferred_element_type=F32).astype(BF16)
    hid = jnp.dot(both[:, channels:], spread, preferred_element_type=F32).astype(BF16)
    shift = pick((128, 256), lambda i, j: j == i + 192)
    gl = jnp.dot(grow(lines[16:24, :128]), shift, preferred_element_type=F32).astype(BF16)
    dims = (((0,), (0,)), ((), ()))
    crit[...] = lax.dot_general(gp, nb, dims, preferred_element_type=F32)
    crit[...] += lax.dot_general(hid, gl, dims, preferred_element_type=F32)

    def pack(z, _):
        for dy, dc, dest in places(parts, yl_ref, zl_ref, core_ref, z):
            piece = crit[pl.ds(pl.multiple_of(dest * padded, 16), padded), :].astype(BF16)
            (sent_ref if dc else kept_ref)[dy, z] = piece
        return 0

    lax.fori_loop(0, n_z, pack, 0)


def places(parts, yl_ref, zl_ref, core_ref, z):
    n_yl, n_zh, n_zl, n_c = parts
    far = lax.div(z, n_zh)
    zl = zl_ref[0] + far * (n_zl - 1 - 2 * zl_ref[0])
    place = (z - far * n_zh) * n_zl + zl
    found = []
    for dy in range(n_yl):
        for dc in range(n_c):
            yl = yl_ref[0] if dy == 0 else n_yl - 1 - yl_ref[0]
            c = core_ref[0] if dc == 0 else n_c - 1 - core_ref[0]
            found.append((dy, dc, (yl * n_zh * n_zl + place) * n_c + c))
    return found


def plus(left, right):
    return (left.astype(F32) + right.astype(F32)).astype(BF16)


def split_kernel(kept_ref, got_ref, own_ref, other_ref):
    own_ref[...] = plus(kept_ref[0], got_ref[0])
    if kept_ref.shape[0] > 1:
        other_ref[...] = plus(kept_ref[1], got_ref[1])


def merge_kernel(has_right, left_ref, *refs):
    right_ref = refs[0] if has_right else None
    crit_ref, *outs = refs[has_right:]
    total = plus(left_ref[...], right_ref[...]) if has_right else left_ref[...]
    width = total.shape[1]
    part = total.shape[0] // len(outs)
    for i, out_ref in enumerate(outs):
        rows = slice(i * part, (i + 1) * part)
        out_ref[:, :width, :] = total[rows]
        out_ref[:, width:, :] = crit_ref[rows]


def add_kernel(left_ref, right_ref, out_ref):
    out_ref[...] = plus(left_ref[...], right_ref[...])


def pick_kernel(targets, sec_ref, moved_ref, held_ref, out_ref):
    gets = functools.reduce(jnp.logical_or, [sec_ref[0] == target for target in targets])

    @pl.when(gets)
    def _():
        out_ref[...] = moved_ref[...]

    @pl.when(jnp.logical_not(gets))
    def _():
        out_ref[...] = held_ref[...]


def finish_kernel(parts, yl_ref, zl_ref, core_ref, xn_ref, g_ref, h_ref, da_ref, *refs):
    outs, (down, up) = refs[:-2], refs[-2:]
    n_yl, n_zh, n_zl, _ = parts
    n_z = n_zh * n_zl
    features = xn_ref.shape[1]
    dims = (((0,), (0,)), ((), ()))
    width = 256
    for k in range(features // width):
        cols = pl.ds(k * width, width)
        down[cols, :] = lax.dot_general(xn_ref[:, cols], da_ref[...], dims, preferred_element_type=F32)
        up[cols, :] = lax.dot_general(g_ref[:, cols], h_ref[...], dims, preferred_element_type=F32)
    span = features // math.prod(parts)

    def pack(z, _):
        for dy, dc, dest in places(parts, yl_ref, zl_ref, core_ref, z):
            rows = pl.ds(pl.multiple_of(dest * span, 8), span)
            piece = jnp.concatenate([down[rows, :], up[rows, :]], axis=0)
            outs[dc * n_yl + dy][z] = piece.astype(BF16)
        return 0

    lax.fori_loop(0, n_z, pack, 0)


def join_kernel(sec_ref, *refs):
    *parts, out_ref = refs
    rows = parts[0].shape[0]

    @pl.when(sec_ref[0] % 2 == 1)
    def _():
        for i, ref in enumerate(parts):
            out_ref[i * rows : (i + 1) * rows, :] = ref[...]


def after(value, token):
    return lax.optimization_barrier((value, token))[0]


def swap(block, axis, size):
    return lax.ppermute(block, axis, [(i, size - 1 - i) for i in range(size)])


def body(parts, *args):
    return whole(parts, *args)


def whole(parts, section_in, top_grad, seq_lengths, lang_labels, norm_gain, w_down, w_up, critic_first, critic_second):
    n_yl, n_zh, n_zl, n_c = parts
    n_z = n_zh * n_zl
    n_dp = n_yl * n_z * n_c
    sec = lax.axis_index(SEC)
    core = lax.axis_index("c")
    micros, seq_len, features = 4, 128, section_in.shape[-1]
    rank = w_down.shape[-1]
    rows = micros * seq_len
    chunks = rows // CHUNK
    x = section_in.reshape(rows, features)
    top = top_grad.reshape(rows, features)
    gain = norm_gain.reshape(1, features)
    wd = w_down[0]
    sec_s = sec.reshape(1).astype(jnp.int32)
    core_s = core.reshape(1).astype(jnp.int32)
    yl_s = lax.axis_index("yl").reshape(1).astype(jnp.int32)
    zl_s = lax.axis_index("zl").reshape(1).astype(jnp.int32)
    channels = critic_first.shape[1]
    half = channels // 2
    sds = jax.ShapeDtypeStruct

    lens = seq_lengths.reshape(micros)
    mine = call(
        half_kernel,
        sds((critic_first.shape[0], half), BF16),
        [SM, VM],
        (core_s, critic_first),
        0,
        1 << 19,
    )
    even = lax.ppermute(mine, SEC, [(i, i + 1) for i in range(0, SECTIONS, 2)])
    second = critic_second.T
    xn, h, a, q, pooled, wut, wdt, grads, inner = call(
        prepare_kernel,
        (
            sds((rows, features), BF16),
            sds((rows, rank), BF16),
            sds((rows, rank), F32),
            sds((rows, 128), F32),
            sds((8, features), F32),
            sds((features, rank), BF16),
            sds((rank, features), BF16),
            sds((rows, features), BF16),
            sds((rows, rank), BF16),
        ),
        [SM] * 4 + [VM] * 4,
        (lens, sec_s, yl_s, zl_s, x, gain, wd, w_up[0]),
        2 * rows * features * rank,
        8 << 20,
    )

    three = SECTIONS // 2 - 1
    held = {}
    band_rows = critic_first.shape[0]
    share = channels // n_dp
    padded = -(-share // 16) * 16

    def join(token, *pieces):
        return call(
            join_kernel,
            sds((len(pieces) * pieces[0].shape[0], half), BF16),
            [SM] + [VM] * len(pieces),
            (after(sec_s, token), *pieces),
            0,
            2 << 20,
        )

    def side_work(step, token):
        if step == 0:
            held["pair"] = join(token, even, mine)
            held["far"] = [lax.ppermute(held["pair"], SEC, [(i, three)]) for i in (7, 5, 1)]
        elif step == 1:
            held["pooled"] = lax.ppermute(after(pooled, token), SEC, [(4, three)])
        elif step == 5:
            far = held["far"]
            held["own"] = join(token, far[2], held["pair"], far[1], far[0])
            pairs = [(three * 2, three * 2 + 1), (three * 2 + 1, three * 2)]
            held["other"] = lax.ppermute(held["own"], SEC + ("c",), pairs)
        elif step == 7:
            held["lines"], held["rev"] = call(
                critic_kernel,
                (sds((32, features), BF16), sds((8, features), F32)),
                [SM] * 4 + [VM] * 4,
                (
                    after(sec_s, token),
                    core_s,
                    lang_labels.reshape(micros),
                    lens,
                    held["pooled"],
                    held["own"],
                    held["other"],
                    second,
                ),
                1 << 27,
                4 << 20,
                scratch=[pltpu.VMEM((32, features), F32)],
            )
        if step in (10, 12, 14) and "moved" in held:
            targets, moved = held.pop("moved")
            held["lines"] = call(
                functools.partial(pick_kernel, targets),
                sds(held["lines"].shape, BF16),
                [SM, VM, VM],
                (after(sec_s, token), moved, held["lines"]),
                0,
                1 << 18,
            )
        if step in (8, 10, 12):
            lines = after(held["lines"], token)
            if step == 8:
                route = [(3, 7)]
            elif step == 10:
                route = [(3, 1), (7, 5)]
            else:
                route = [(i + 1, i) for i in range(0, SECTIONS, 2)]
            moved = lax.ppermute(lines, SEC, route)
            held["moved"] = ([target for _, target in route], moved)
        elif step == 15:
            kept, sent = call(
                functools.partial(critic_sums_kernel, band_rows, parts),
                (sds((n_yl, n_z, padded, rank), BF16),) * 2,
                [SM, SM, SM, SM, VM],
                (after(sec_s, token), yl_s, zl_s, core_s, held["lines"]),
                1 << 26,
                1 << 20,
                scratch=[pltpu.VMEM((n_dp * padded, rank), F32)],
            )
            held["kept"] = kept
            held["got"] = swap(sent, "c", n_c)
        elif step == 17:
            one = sds((n_z, padded, rank), BF16)
            own, other = call(
                split_kernel, (one, one), [VM, VM], (after(held["kept"], token), held["got"]), 0, 1 << 20
            )
            held["own_sum"] = own
            if n_yl == 2:
                held["other_sum"] = swap(other, "yl", n_yl)
        elif step == 19 and n_yl == 2:
            args = (after(held["own_sum"], token), held["other_sum"])
            held["own_sum"] = call(add_kernel, sds(args[0].shape, BF16), [VM, VM], args, 0, 1 << 20)

    steps = DELAY * (SECTIONS - 1) + chunks
    received = {}
    relay_route = [(i, i - 1) for i in range(1, SECTIONS)]
    for step in range(steps):
        has_top = step < chunks
        has_in = step >= DELAY
        first_rev = DELAY * (SECTIONS - 1 - three)
        has_rev = first_rev <= step < first_rev + chunks
        args = [sec_s, lens, x, a, q, gain, wut, wdt]
        specs = [SM, SM] + [VM] * 6
        if has_top:
            args.append(top)
        if has_in:
            args.append(received.pop(step - DELAY))
        if has_rev:
            args.append(held["rev"])
        args += [grads, inner]
        specs += [VM] * (len(args) - len(specs))
        passed = [len(args) - 2, len(args) - 1] + STAY
        outgoing, grads, inner, *stay = call(
            functools.partial(step_kernel, step, chunks, has_top, has_in, has_rev),
            (sds((CHUNK, features), BF16),) + tuple(sds(args[i].shape, args[i].dtype) for i in passed),
            specs,
            tuple(args),
            4 * CHUNK * features * rank,
            3 << 20,
            aliases={i: k + 1 for k, i in enumerate(passed)},
        )
        x, a, q, wut, wdt = stay
        if step < steps - DELAY:
            received[step] = lax.ppermute(outgoing, SEC, relay_route)
        side_work(step, outgoing)

    span = features // n_dp
    piece = sds((n_z, 2 * span, rank), BF16)
    packed = call(
        functools.partial(finish_kernel, parts),
        (piece,) * (n_yl * n_c),
        [SM] * 3 + [VM] * 4,
        (yl_s, zl_s, core_s, xn, grads, h, inner),
        4 * rows * features * rank,
        8 << 20,
        scratch=[pltpu.VMEM((features, rank), F32)] * 2,
    )

    kept, sent = packed[:n_yl], packed[n_yl:]
    halves = [None] * n_yl
    for i in reversed(range(n_yl)):
        arrived = swap(sent[i], "c", n_c)
        args = (kept[i], arrived)
        halves[i] = call(add_kernel, sds(arrived.shape, BF16), [VM, VM], args, 0, 2 << 20)
    args = [halves[0]]
    if n_yl == 2:
        args.append(swap(halves[1], "yl", n_yl))
    args.append(held["own_sum"])
    share_rows = 2 * span + padded
    pieces = call(
        functools.partial(merge_kernel, n_yl == 2),
        (sds((n_zh, share_rows, rank), BF16),) * n_zl,
        [VM] * len(args),
        tuple(args),
        0,
        4 << 20,
    )
    summed = pieces[0]
    if n_zl == 2:
        arrived = swap(pieces[1], "zl", n_zl)
        summed = call(add_kernel, sds(arrived.shape, BF16), [VM, VM], (summed, arrived), 0, 2 << 20)
    if n_zh > 1:
        summed = lax.all_to_all(summed, "zh", 0, 0, tiled=True)
    total = jnp.sum(summed.astype(F32), axis=0)
    down = total[:span]
    up = total[span : 2 * span].T
    crit = total[2 * span : 2 * span + share]
    dp_place = lax.axis_index(("yl", "zh", "zl", "c"))
    wd_own = lax.dynamic_slice_in_dim(wd, dp_place * span, span, 0).astype(F32)
    gain_own = lax.dynamic_slice_in_dim(gain[0], dp_place * span, span, 0)
    grad_gain = jnp.sum(down * wd_own, axis=1) / gain_own
    first = crit[:, :band_rows].T
    second_grad = crit[:, 192 : 192 + critic_second.shape[1]]
    return (down[None], up[None], grad_gain[None], first, second_grad)


def solution(mesh):
    n_dp = mesh.shape["dp"]
    parts = (2, n_dp // 4, 1, 2) if n_dp >= 4 else (1, n_dp // 2, 1, 2)
    fine = Mesh(mesh.devices.reshape((SECTIONS // 2, 2) + parts), SEC + ("yl", "zh", "zl", "c"))
    dp = ("yl", "zh", "zl", "c")
    return jax.shard_map(
        functools.partial(body, parts),
        mesh=fine,
        in_specs=(
            P(SEC, None, dp, None, None),
            P(None, dp, None, None),
            P(None, dp),
            P(None, dp),
            P(SEC, None),
            P(SEC, None, None),
            P(SEC, None, None),
            P(SEC, None),
            P(),
        ),
        out_specs=(P(SEC, dp, None), P(SEC, None, dp), P(SEC, dp), P(SEC, dp), P(dp, None)),
        check_vma=False,
    )
```

```python
import functools
import math

import jax
import jax.numpy as jnp
from jax import lax
from jax.experimental import pallas as pl
from jax.experimental.pallas import tpu as pltpu
from jax.sharding import Mesh, PartitionSpec as P


EPSILON = 1e-06
REVERSAL = 0.5
SECTIONS = 8
CHUNK = 64
STAY = [2, 3, 4, 6, 7]
DELAY = 2
SEC = ("x", "yh")
F32 = jnp.float32
BF16 = jnp.bfloat16
VM = pl.BlockSpec(memory_space=pltpu.VMEM)
SM = pl.BlockSpec(memory_space=pltpu.SMEM)


def silu_slope(pre_act):
    sigma = jax.nn.sigmoid(pre_act)
    return sigma * (1.0 + pre_act * (1.0 - sigma))


def call(kernel, out_shape, in_specs, args, flops, moved, aliases=None, scratch=(), limit=16):
    return pl.pallas_call(
        kernel,
        out_shape=out_shape,
        in_specs=in_specs,
        out_specs=jax.tree.map(lambda _: VM, out_shape),
        input_output_aliases=aliases or {},
        scratch_shapes=scratch,
        compiler_params=pltpu.CompilerParams(vmem_limit_bytes=limit << 20),
        cost_estimate=pl.CostEstimate(flops=flops, bytes_accessed=moved, transcendentals=0),
    )(*args)


def half_kernel(core_ref, first_ref, mine_ref):
    half = mine_ref.shape[1]
    for c in range(2):

        @pl.when(core_ref[0] == c)
        def _():
            mine_ref[...] = first_ref[:, c * half : (c + 1) * half]


def prepare_kernel(lens_ref, _sec, _yl, _zl, x_ref, gain_ref, wd_ref, wu_ref, *refs):
    xn_ref, h_ref, a_ref, q_ref, pooled_ref, wut_ref, wdt_ref, _, _ = refs
    micros, seq_len = 4, 128
    gain = gain_ref[0:1, :]
    wut_ref[...] = wu_ref[...].T
    wdt_ref[...] = wd_ref[...].T
    pooled_ref[...] = jnp.zeros_like(pooled_ref)
    positions = lax.broadcasted_iota(jnp.int32, (seq_len, 1), 0)
    for m in range(micros):
        rows = pl.ds(m * seq_len, seq_len)
        values = x_ref[rows, :].astype(F32)
        count = lens_ref[m]
        total = jnp.sum(jnp.where(positions < count, values, 0.0), axis=0, keepdims=True)
        pooled_ref[m : m + 1, :] = total / count.astype(F32)
        q = lax.rsqrt(jnp.mean(values * values, axis=-1, keepdims=True) + EPSILON)
        normed = (values * q * gain).astype(BF16)
        xn_ref[rows, :] = normed
        a = jnp.dot(normed, wd_ref[...], preferred_element_type=F32)
        a_ref[rows, :] = a
        h_ref[rows, :] = (a * jax.nn.sigmoid(a)).astype(BF16)
        q_ref[rows, :] = jnp.broadcast_to(q, (seq_len, 128))


def step_kernel(step, chunks, has_top, has_in, has_rev, *refs):
    refs = list(refs)
    sec_ref, lens_ref, x_ref, a_ref, q_ref, gain_ref, wut_ref, wdt_ref = refs[:8]
    refs = refs[8:]
    top_ref = refs.pop(0) if has_top else None
    in_ref = refs.pop(0) if has_in else None
    rev_ref = refs.pop(0) if has_rev else None
    out_ref, g_ref, da_ref = refs[2:5]
    features = x_ref.shape[1]
    sec = sec_ref[0]
    place = step - DELAY * (SECTIONS - 1 - sec)
    live = (place >= 0) & (place < chunks)
    place = jnp.clip(place, 0, chunks - 1)
    rows = pl.ds(pl.multiple_of(place * CHUNK, CHUNK), CHUNK)

    if has_top:

        @pl.when(live & (sec == SECTIONS - 1))
        def _():
            g_ref[rows, :] = top_ref[rows, :]

    if has_in:

        @pl.when(live & (sec < SECTIONS - 1))
        def _():
            g_ref[rows, :] = in_ref[...]

    if has_rev:

        @pl.when(live & (sec == SECTIONS // 2 - 1))
        def _():
            per = 128 // CHUNK
            micro = lax.div(place, per)
            first = lax.rem(place, per) * CHUNK
            positions = lax.broadcasted_iota(jnp.int32, (CHUNK, 1), 0) + first
            extra = jnp.where(positions < lens_ref[micro], rev_ref[pl.ds(micro, 1), :], 0.0)
            g_ref[rows, :] = (in_ref[...].astype(F32) + extra).astype(BF16)

    @pl.when(live)
    def _():
        g = g_ref[rows, :]
        a = a_ref[rows, :]
        q = q_ref[rows, 0:1]
        dh = jnp.dot(g, wut_ref[...], preferred_element_type=F32)
        da = (dh * silu_slope(a)).astype(BF16)
        da_ref[rows, :] = da
        mean = jnp.sum(da.astype(F32) * a, axis=-1, keepdims=True) * (1.0 / features)
        dxn = jnp.dot(da, wdt_ref[...], preferred_element_type=F32)
        x = x_ref[rows, :].astype(F32)
        out = g.astype(F32) + q * (dxn * gain_ref[0:1, :]) - x * (q * q * mean)
        out_ref[...] = out.astype(BF16)


def per_row(ref, shape):
    rows = lax.broadcasted_iota(jnp.int32, shape, 0)
    column = jnp.ones(shape, jnp.int32)
    for m in range(4):
        column = jnp.where(rows == m, ref[m], column)
    return column


def critic_kernel(
    sec_ref, core_ref, labels_ref, lens_ref, pooled_ref, own_ref, other_ref, second_ref, lines_ref, rev_ref, hold
):
    half = own_ref.shape[1]
    channels = 2 * half
    languages = second_ref.shape[0]

    @pl.when(sec_ref[0] == SECTIONS // 2 - 1)
    def _():
        pooled = pooled_ref[...].astype(BF16).astype(F32)
        r = lax.rsqrt(jnp.mean(pooled * pooled, axis=-1, keepdims=True) + EPSILON)
        unit = pooled * r
        normed = unit.astype(BF16)
        core = core_ref[0]
        pre_own = jnp.dot(normed, own_ref[...], preferred_element_type=F32)
        pre_other = jnp.dot(normed, other_ref[...], preferred_element_type=F32)
        low = jnp.where(core == 0, pre_own, pre_other)
        high = jnp.where(core == 0, pre_other, pre_own)
        pre = jnp.concatenate([low, high], axis=1)
        hidden = (pre * jax.nn.sigmoid(pre)).astype(BF16)
        second = second_ref[...]
        dims = (((1,), (1,)), ((), ()))
        logits = lax.dot_general(hidden, second, dims, preferred_element_type=F32)
        exponent = jnp.exp(logits)
        probs = exponent / jnp.sum(exponent, axis=-1, keepdims=True)
        lanes = lax.broadcasted_iota(jnp.int32, logits.shape, 1)
        onehot = jnp.where(lanes == per_row(labels_ref, logits.shape), 1.0, 0.0)
        valid = lax.broadcasted_iota(jnp.int32, logits.shape, 0) < 4
        grad_logits = jnp.where(valid, probs - onehot, 0.0).astype(BF16)
        grad_hidden = jnp.dot(grad_logits, second, preferred_element_type=F32)
        grad_pre = (grad_hidden * silu_slope(pre)).astype(BF16)
        hold[...] = jnp.zeros_like(hold)
        hold[0:8, :] = normed.astype(F32)
        hold[8:16, 0:channels] = grad_pre.astype(F32)
        hold[8:16, channels:] = hidden.astype(F32)
        hold[16:24, 0:languages] = grad_logits.astype(F32)
        lines_ref[...] = hold[...].astype(BF16)
        low = grad_pre[:, :half]
        high = grad_pre[:, half:]
        mine = jnp.where(core == 0, low, high)
        theirs = jnp.where(core == 0, high, low)
        grad_normed = lax.dot_general(mine, own_ref[...], dims, preferred_element_type=F32)
        grad_normed += lax.dot_general(theirs, other_ref[...], dims, preferred_element_type=F32)
        mean = jnp.mean(grad_normed * unit, axis=-1, keepdims=True)
        grad_pooled = r * (grad_normed - unit * mean)
        rev_ref[...] = -REVERSAL * grad_pooled / per_row(lens_ref, (8, 1)).astype(F32)


def critic_sums_kernel(band_rows, parts, sec_ref, yl_ref, z_ref, core_ref, lines_ref, kept_ref, sent_ref, crit):
    n_dp = math.prod(parts)
    n_z = parts[1]
    features = lines_ref.shape[1]
    channels = features // 2
    padded = crit.shape[0] // n_dp
    share = channels // n_dp

    def grow(block):
        return jnp.concatenate([block, jnp.zeros_like(block)], axis=0).astype(BF16)

    def pick(shape, test):
        rows = lax.broadcasted_iota(jnp.int32, shape, 0)
        columns = lax.broadcasted_iota(jnp.int32, shape, 1)
        return jnp.where(test(rows, columns), 1.0, 0.0).astype(BF16)

    lines = lines_ref[...].astype(F32)
    base = sec_ref[0] * band_rows
    band = pick((features, 256), lambda i, j: (i == j + base) & (j < band_rows))
    nb = jnp.dot(grow(lines[0:8]), band, preferred_element_type=F32).astype(BF16)
    wide = (channels, n_dp * padded)
    columns = lax.broadcasted_iota(jnp.int32, (1, wide[1]), 1)
    slot = lax.div(columns, padded)
    inside = columns - slot * padded
    source = jnp.where(inside < share, slot * share + inside, -1)
    spread = jnp.where(lax.broadcasted_iota(jnp.int32, wide, 0) == source, 1.0, 0.0).astype(BF16)
    both = grow(lines[8:16])
    gp = jnp.dot(both[:, :channels], spread, preferred_element_type=F32).astype(BF16)
    hid = jnp.dot(both[:, channels:], spread, preferred_element_type=F32).astype(BF16)
    shift = pick((128, 256), lambda i, j: j == i + 192)
    gl = jnp.dot(grow(lines[16:24, :128]), shift, preferred_element_type=F32).astype(BF16)
    dims = (((0,), (0,)), ((), ()))
    crit[...] = lax.dot_general(gp, nb, dims, preferred_element_type=F32)
    crit[...] += lax.dot_general(hid, gl, dims, preferred_element_type=F32)

    for i in range(n_z):
        for dy, dc, dest in places(parts, yl_ref, core_ref, jnp.bitwise_xor(z_ref[0], i)):
            piece = crit[pl.ds(pl.multiple_of(dest * padded, 16), padded), :].astype(BF16)
            (sent_ref if dc else kept_ref)[dy, i] = piece


def places(parts, yl_ref, core_ref, z):
    n_yl, n_z, n_c = parts
    found = []
    for dy in range(n_yl):
        for dc in range(n_c):
            yl = yl_ref[0] if dy == 0 else n_yl - 1 - yl_ref[0]
            c = core_ref[0] if dc == 0 else n_c - 1 - core_ref[0]
            found.append((dy, dc, (yl * n_z + z) * n_c + c))
    return found


def plus(left, right):
    return (left.astype(F32) + right.astype(F32)).astype(BF16)


def split_kernel(kept_ref, got_ref, own_ref, other_ref):
    own_ref[...] = plus(kept_ref[0], got_ref[0])
    if kept_ref.shape[0] > 1:
        other_ref[...] = plus(kept_ref[1], got_ref[1])


def fold_kernel(left_ref, right_ref, low_ref, high_ref):
    total = plus(left_ref[...], right_ref[...])
    half = low_ref.shape[0]
    low_ref[...] = total[:half]
    high_ref[...] = total[half:]


def add_kernel(left_ref, right_ref, out_ref):
    out_ref[...] = plus(left_ref[...], right_ref[...])


def pick_kernel(targets, sec_ref, moved_ref, held_ref, out_ref):
    gets = functools.reduce(jnp.logical_or, [sec_ref[0] == target for target in targets])

    @pl.when(gets)
    def _():
        out_ref[...] = moved_ref[...]

    @pl.when(jnp.logical_not(gets))
    def _():
        out_ref[...] = held_ref[...]


def finish_kernel(parts, yl_ref, core_ref, xn_ref, g_ref, h_ref, da_ref, *refs):
    outs, (down, up) = refs[:-2], refs[-2:]
    n_yl, n_z, _ = parts
    features = xn_ref.shape[1]
    dims = (((0,), (0,)), ((), ()))
    width = 256
    for k in range(features // width):
        cols = pl.ds(k * width, width)
        down[cols, :] = lax.dot_general(xn_ref[:, cols], da_ref[...], dims, preferred_element_type=F32)
        up[cols, :] = lax.dot_general(g_ref[:, cols], h_ref[...], dims, preferred_element_type=F32)
    span = features // math.prod(parts)

    def pack(z, _):
        for dy, dc, dest in places(parts, yl_ref, core_ref, z):
            rows = pl.ds(pl.multiple_of(dest * span, 8), span)
            piece = jnp.concatenate([down[rows, :], up[rows, :]], axis=0)
            outs[dc * n_yl + dy][z] = piece.astype(BF16)
        return 0

    lax.fori_loop(0, n_z, pack, 0)


def join_kernel(sec_ref, *refs):
    *parts, out_ref = refs
    rows = parts[0].shape[0]

    @pl.when(sec_ref[0] % 2 == 1)
    def _():
        for i, ref in enumerate(parts):
            out_ref[i * rows : (i + 1) * rows, :] = ref[...]


def after(value, token):
    return lax.optimization_barrier((value, token))[0]


def swap(block, axis, size):
    return lax.ppermute(block, axis, [(i, size - 1 - i) for i in range(size)])


def body(parts, *args):
    return whole(parts, *args)


def whole(parts, section_in, top_grad, seq_lengths, lang_labels, norm_gain, w_down, w_up, critic_first, critic_second):
    n_yl, n_z, n_c = parts
    n_dp = n_yl * n_z * n_c
    sec = lax.axis_index(SEC)
    core = lax.axis_index("c")
    micros, seq_len, features = 4, 128, section_in.shape[-1]
    rank = w_down.shape[-1]
    rows = micros * seq_len
    chunks = rows // CHUNK
    x = section_in.reshape(rows, features)
    top = top_grad.reshape(rows, features)
    gain = norm_gain.reshape(1, features)
    wd = w_down[0]
    sec_s = sec.reshape(1).astype(jnp.int32)
    core_s = core.reshape(1).astype(jnp.int32)
    yl_s = lax.axis_index("yl").reshape(1).astype(jnp.int32)
    z_s = lax.axis_index("z").reshape(1).astype(jnp.int32)
    channels = critic_first.shape[1]
    half = channels // 2
    sds = jax.ShapeDtypeStruct

    lens = seq_lengths.reshape(micros)
    mine = call(
        half_kernel,
        sds((critic_first.shape[0], half), BF16),
        [SM, VM],
        (core_s, critic_first),
        0,
        1 << 19,
    )
    even = lax.ppermute(mine, SEC, [(i, i + 1) for i in range(0, SECTIONS, 2)])
    second = critic_second.T
    xn, h, a, q, pooled, wut, wdt, grads, inner = call(
        prepare_kernel,
        (
            sds((rows, features), BF16),
            sds((rows, rank), BF16),
            sds((rows, rank), F32),
            sds((rows, 128), F32),
            sds((8, features), F32),
            sds((features, rank), BF16),
            sds((rank, features), BF16),
            sds((rows, features), BF16),
            sds((rows, rank), BF16),
        ),
        [SM] * 4 + [VM] * 4,
        (lens, sec_s, yl_s, z_s, x, gain, wd, w_up[0]),
        2 * rows * features * rank,
        8 << 20,
    )

    three = SECTIONS // 2 - 1
    held = {}
    band_rows = critic_first.shape[0]
    share = channels // n_dp
    padded = -(-share // 16) * 16

    def join(token, *pieces):
        return call(
            join_kernel,
            sds((len(pieces) * pieces[0].shape[0], half), BF16),
            [SM] + [VM] * len(pieces),
            (after(sec_s, token), *pieces),
            0,
            2 << 20,
        )

    def side_work(step, token):
        if step == 0:
            held["pair"] = join(token, even, mine)
            held["far"] = [lax.ppermute(held["pair"], SEC, [(i, three)]) for i in (7, 5, 1)]
        elif step == 1:
            held["pooled"] = lax.ppermute(after(pooled, token), SEC, [(4, three)])
        elif step == 5:
            far = held["far"]
            held["own"] = join(token, far[2], held["pair"], far[1], far[0])
            pairs = [(three * 2, three * 2 + 1), (three * 2 + 1, three * 2)]
            held["other"] = lax.ppermute(held["own"], SEC + ("c",), pairs)
        elif step == 7:
            held["lines"], held["rev"] = call(
                critic_kernel,
                (sds((32, features), BF16), sds((8, features), F32)),
                [SM] * 4 + [VM] * 4,
                (
                    after(sec_s, token),
                    core_s,
                    lang_labels.reshape(micros),
                    lens,
                    held["pooled"],
                    held["own"],
                    held["other"],
                    second,
                ),
                1 << 27,
                4 << 20,
                scratch=[pltpu.VMEM((32, features), F32)],
            )
        if step in (10, 12, 14) and "moved" in held:
            targets, moved = held.pop("moved")
            held["lines"] = call(
                functools.partial(pick_kernel, targets),
                sds(held["lines"].shape, BF16),
                [SM, VM, VM],
                (after(sec_s, token), moved, held["lines"]),
                0,
                1 << 18,
            )
        if step in (8, 10, 12):
            lines = after(held["lines"], token)
            if step == 8:
                route = [(3, 7)]
            elif step == 10:
                route = [(3, 1), (7, 5)]
            else:
                route = [(i + 1, i) for i in range(0, SECTIONS, 2)]
            moved = lax.ppermute(lines, SEC, route)
            held["moved"] = ([target for _, target in route], moved)
        elif step == 14:
            kept, sent = call(
                functools.partial(critic_sums_kernel, band_rows, parts),
                (sds((n_yl, n_z, padded, rank), BF16),) * 2,
                [SM, SM, SM, SM, VM],
                (after(sec_s, token), yl_s, z_s, core_s, held["lines"]),
                1 << 26,
                1 << 20,
                scratch=[pltpu.VMEM((n_dp * padded, rank), F32)],
            )
            held["kept"] = kept
            held["got"] = swap(sent, "c", n_c)
        elif step == 16:
            one = sds((n_z, padded, rank), BF16)
            own, other = call(split_kernel, (one, one), [VM, VM], (after(held["kept"], token), held["got"]), 0, 1 << 20)
            held["own_sum"] = own
            if n_yl == 2:
                held["other_sum"] = swap(other, "yl", n_yl)
        elif step == 18 and n_yl == 2:
            fold(after(held["own_sum"], token), held["other_sum"], n_z // 2)

    def fold(left, right, bit):
        size = left.shape[0]
        if size == 1:
            held["own_sum"] = call(add_kernel, sds(left.shape, BF16), [VM, VM], (left, right), 0, 1 << 18)
            return
        one = sds((size // 2,) + left.shape[1:], BF16)
        held["own_sum"], high = call(fold_kernel, (one, one), [VM, VM], (left, right), 0, 1 << 20)
        held["other_sum"] = lax.ppermute(high, "z", [(i, i ^ bit) for i in range(n_z)])

    steps = DELAY * (SECTIONS - 1) + chunks
    received = {}
    relay_route = [(i, i - 1) for i in range(1, SECTIONS)]
    for step in range(steps):
        has_top = step < chunks
        has_in = step >= DELAY
        first_rev = DELAY * (SECTIONS - 1 - three)
        has_rev = first_rev <= step < first_rev + chunks
        args = [sec_s, lens, x, a, q, gain, wut, wdt]
        specs = [SM, SM] + [VM] * 6
        if has_top:
            args.append(top)
        if has_in:
            args.append(received.pop(step - DELAY))
        if has_rev:
            args.append(held["rev"])
        args += [grads, inner]
        specs += [VM] * (len(args) - len(specs))
        passed = [len(args) - 2, len(args) - 1] + STAY
        outgoing, grads, inner, *stay = call(
            functools.partial(step_kernel, step, chunks, has_top, has_in, has_rev),
            (sds((CHUNK, features), BF16),) + tuple(sds(args[i].shape, args[i].dtype) for i in passed),
            specs,
            tuple(args),
            4 * CHUNK * features * rank,
            3 << 20,
            aliases={i: k + 1 for k, i in enumerate(passed)},
        )
        x, a, q, wut, wdt = stay
        if step < steps - DELAY:
            received[step] = lax.ppermute(outgoing, SEC, relay_route)
        side_work(step, outgoing)

    span = features // n_dp
    piece = sds((n_z, 2 * span, rank), BF16)
    packed = call(
        functools.partial(finish_kernel, parts),
        (piece,) * (n_yl * n_c),
        [SM] * 2 + [VM] * 4,
        (yl_s, core_s, xn, grads, h, inner),
        4 * rows * features * rank,
        8 << 20,
        scratch=[pltpu.VMEM((features, rank), F32)] * 2,
    )

    kept, sent = packed[:n_yl], packed[n_yl:]
    halves = [None] * n_yl
    for i in reversed(range(n_yl)):
        arrived = swap(sent[i], "c", n_c)
        args = (kept[i], arrived)
        halves[i] = call(add_kernel, sds(arrived.shape, BF16), [VM, VM], args, 0, 2 << 20)
    summed = halves[0]
    if n_yl == 2:
        arrived = swap(halves[1], "yl", n_yl)
        bit = n_z // 2
        while bit:
            bit //= 2
            fold(held["own_sum"], held["other_sum"], bit)
        summed = call(add_kernel, sds(arrived.shape, BF16), [VM, VM], (summed, arrived), 0, 2 << 20)
    if n_z > 1:
        summed = lax.all_to_all(summed, "z", 0, 0, tiled=True)
    total = jnp.sum(summed.astype(F32), axis=0)
    down = total[:span]
    up = total[span:].T
    crit = held["own_sum"][0, :share].astype(F32)
    dp_place = lax.axis_index(("yl", "z", "c"))
    wd_own = lax.dynamic_slice_in_dim(wd, dp_place * span, span, 0).astype(F32)
    gain_own = lax.dynamic_slice_in_dim(gain[0], dp_place * span, span, 0)
    grad_gain = jnp.sum(down * wd_own, axis=1) / gain_own
    first = crit[:, :band_rows].T
    second_grad = crit[:, 192 : 192 + critic_second.shape[1]]
    return (down[None], up[None], grad_gain[None], first, second_grad)


def solution(mesh):
    n_dp = mesh.shape["dp"]
    parts = (2, n_dp // 4, 2) if n_dp >= 4 else (1, n_dp // 2, 2)
    fine = Mesh(mesh.devices.reshape((SECTIONS // 2, 2) + parts), SEC + ("yl", "z", "c"))
    dp = ("yl", "z", "c")
    return jax.shard_map(
        functools.partial(body, parts),
        mesh=fine,
        in_specs=(
            P(SEC, None, dp, None, None),
            P(None, dp, None, None),
            P(None, dp),
            P(None, dp),
            P(SEC, None),
            P(SEC, None, None),
            P(SEC, None, None),
            P(SEC, None),
            P(),
        ),
        out_specs=(P(SEC, dp, None), P(SEC, None, dp), P(SEC, dp), P(SEC, dp), P(dp, None)),
        check_vma=False,
    )
```
